32 devices in a mesh: section: 2 (over core), req: 4 (over z), head: 4 (over y, x).
Axes of the slice: x: 2, y: 2, z: 4, core: 2. Of those that a mesh axis runs over, the one named last changes fastest.
Arguments:
- tokens: bfloat16 [128, 1024], P('req'), may hold values from -60 to 60, as said below
- deal: int32 [128], P('req'), may hold values from 0 to 127, each once
- lengths: int32 [2, 128], P('section', 'req'), may hold values from 2 to 256, as said below
- cache_keys: bfloat16 [2, 128, 256, 1024], P('section', 'req', None, 'head'), may hold values from -1024 to 1024
- cache_values: bfloat16 [2, 128, 256, 1024], P('section', 'req', None, 'head'), may hold values from -6 to 6
- w_qkv: bfloat16 [2, 1024, 3, 1024], P('section', None, None, 'head'), may hold values from -0.1875 to 0.1875
- w_out: bfloat16 [2, 1024, 1024], P('section', 'head'), may hold values from -0.1875 to 0.1875
- attn_gain: float32 [2, 1024], P('section'), may hold values from 0.5 to 1.5
- ffn_gain: float32 [2, 1024], P('section'), may hold values from 0.5 to 1.5
- w_gate: bfloat16 [2, 1024, 45056], P('section', None, ('req', 'head')), may hold values from -0.1875 to 0.1875
- w_up: bfloat16 [2, 1024, 45056], P('section', None, ('req', 'head')), may hold values from -0.1875 to 0.1875
- w_down: bfloat16 [2, 45056, 1024], P('section', ('req', 'head')), may hold values from -0.109375 to 0.109375
- routes: int32 [2, 128, 2], P('section', 'req'), may hold values from 0 to 15, all different within a row; in each aligned block of 16 rows (0 to 15, 16 to 31, ..., all dimensions but the last counted through in order) at most 4 rows name the same one
- gates: bfloat16 [2, 128, 2], P('section', 'req'), may hold values from 0.25 to 1
Outputs:
- layer_out: bfloat16 [2, 128, 1024], P('section', 'req')
The draws below stay inside these ranges and needn't reach their ends.
Inputs may be any that keep to these rules, and one draw needn't show every extreme that they name: `tokens`: hidden states with row and feature scales that differ. `deal`: each of 0 to 127 appears once. `lengths`: in each layer, one of the 32 slots of each index of req holds a length of exactly 256; the others are anywhere from 2 to 256. `routes`: the two experts of a slot differ; in each aligned block of 16 slots of one layer no expert is named more than 4 times.
All inputs are finite; a program needn't handle non-finite values.
Results may differ from the reference program's by a relative error of at most 0.0053.
Values may be sent and summed in bfloat16 or wider, within the bound.
A program may use at most 128 MiB of HBM per device.

```python
import math
import jax
import jax.numpy as jnp
import numpy as np
from jax import lax

D = 1024
HEADS = 16
HEAD_DIM = 64
EXPERTS = 16
FF = 2816
REQ_DEV = 32
CONTEXT = 256
REQS = 128
BLOCK_ROWS = 16
CAPACITY = 4
N_SECTION = 2


def draw_tokens(key, part):
    key_a, key_b, key_c = jax.random.split(key, 3)
    values = jnp.clip(jax.random.normal(key_a, (REQS, D), jnp.float32), -6.0, 6.0)
    row_scale = jnp.exp(jax.random.uniform(key_b, (REQS, 1), jnp.float32, 0.0, 2.302585))
    col_scale = jnp.exp(jax.random.uniform(key_c, (1, D), jnp.float32, 0.0, 2.302585))
    return (values * row_scale * col_scale * 0.1).astype(jnp.bfloat16)


def draw_lengths(key, part):
    key_a, key_b = jax.random.split(key)
    uniform_lengths = jax.random.randint(key_a, (N_SECTION, REQS), 2, CONTEXT + 1)
    longest = jax.random.randint(key_b, (N_SECTION, REQS // REQ_DEV, 1), 0, REQ_DEV)
    offsets = jnp.arange(REQ_DEV).reshape(1, 1, REQ_DEV)
    marked = (offsets == longest).reshape(N_SECTION, REQS)
    return jnp.where(marked, CONTEXT, uniform_lengths).astype(jnp.int32)


def draw_cache_keys(key, part):
    key_a = jax.random.fold_in(key, 0)
    full_shape = (N_SECTION, REQS, CONTEXT, HEADS * HEAD_DIM)
    values = jnp.clip(jax.random.normal(key_a, full_shape, jnp.float32), -6.0, 6.0)
    return jnp.clip(values, -1024.0, 1024.0).astype(jnp.bfloat16)


def block_scale(rng, dims, cuts, low, top_value):
    gain, own = 1.0, jax.random.fold_in(rng, 6)
    for axis_at, shards_of in cuts:
        steps = jnp.exp(jax.random.uniform(jax.random.fold_in(own, axis_at), (shards_of,), jnp.float32, low / len(cuts), top_value / len(cuts)))
        gain = gain * jnp.repeat(steps, dims[axis_at] // shards_of).reshape([-1 if axis == axis_at else 1 for axis in range(len(dims))])
    return gain


def assign_block(own_key, own, number, rows, count, top, most, lean):
    sequence = jax.random.permutation(own_key, count)
    crowded, ordinary = load_shares(count, rows * top, most, lean, True), load_shares(count, rows * top, most, lean, False)
    places = jnp.arange(count)

    def named(sizes, offset_by):
        used = int((sizes > 0).sum())
        fixed = max(1, used // 4)
        passed = fixed + (places - fixed + offset_by * (used - fixed)) % max(1, count - fixed)
        return jnp.zeros((count,), jnp.int32).at[sequence[jnp.where(places < fixed, places, passed)]].set(jnp.asarray(sizes, jnp.int32))

    sizes = jnp.where(number % 4 == 0, named(crowded, number // 4), named(ordinary, number - number // 4 - 1))
    mixed = jax.random.permutation(jax.random.fold_in(own, 3), count)
    source_of, receiver = mixed[0:count // 2 * 2:2], mixed[1:count // 2 * 2:2]
    room = jnp.minimum(sizes[source_of] - 1, most - sizes[receiver]) // 2
    room = jnp.where((source_of == sequence[0]) | (receiver == sequence[0]) | (sizes[receiver] == 0), 0, jnp.maximum(room, 0))
    passed = jax.random.randint(jax.random.fold_in(own, 4), (count // 2,), 0, 1 << 20) % (room + 1)
    sizes = sizes.at[source_of].add(-passed).at[receiver].add(passed)
    items = jnp.searchsorted(jnp.cumsum(sizes), jnp.arange(rows * top), side="right").astype(jnp.int32)
    table = items.reshape(top, rows).T
    table = table[jax.random.permutation(jax.random.fold_in(own, 1), rows)]
    offset_by = jax.random.randint(jax.random.fold_in(own, 2), (rows, 1), 0, top)
    return jnp.take_along_axis(table, (jnp.arange(top)[None, :] + offset_by) % top, axis=1)


def load_shares(amount, total, bound, slope, full):
    weights = [(1 << 20) // math.isqrt(standing ** slope) + 1 for standing in range(1, amount + 1)]
    largest = bound if full else min(bound, max(-(-total // amount), total * weights[0] // sum(weights)))
    least = 1 if total - largest >= amount - 1 else 0
    given, spare = [largest] + [least] * (amount - 1), total - largest - least * (amount - 1)
    while spare > 0:
        free = [i for i in range(1, amount) if given[i] < largest] or [i for i in range(1, amount) if given[i] < bound]
        whole, budget = sum([weights[i] for i in free]), spare
        for i in free:
            extra = min(bound - given[i], max(1, budget * weights[i] // whole), spare)
            given[i] = given[i] + extra
            spare = spare - extra
    return np.array(given)


def bell_draw(key, dims, spread, bound, shards=(), kind=jnp.bfloat16):
    values = jax.random.normal(key, dims, jnp.float32) * spread
    if len(shards) > 0:
        values = block_scale(key, dims, shards, -0.22, 0.18) * values
    return jnp.clip(values, min=-bound, max=bound).astype(kind)


def setup_inputs(seed: int = 0) -> dict:
    key_list = jax.random.split(jax.random.key(seed), 15)
    tokens = draw_tokens(jax.random.fold_in(key_list[14], 71), 0)
    deal = jax.random.permutation(key_list[1], REQS).astype(jnp.int32)
    lengths = draw_lengths(jax.random.fold_in(key_list[14], 71), 0)
    cache_keys = draw_cache_keys(jax.random.fold_in(key_list[14], 71), 0)
    cache_values = bell_draw(key_list[4], (N_SECTION, REQS, CONTEXT, HEADS * HEAD_DIM), 1.0, 6.0, ((0, 2), (1, 4), (3, 4)))
    w_qkv = bell_draw(key_list[5], (N_SECTION, D, 3, HEADS * HEAD_DIM), D ** -0.5, 0.1875, ((0, 2), (3, 4)))
    w_out = bell_draw(key_list[6], (N_SECTION, HEADS * HEAD_DIM, D), (HEADS * HEAD_DIM) ** -0.5, 0.1875, ((0, 2), (1, 4)))
    attn_gain = jnp.clip(0.5 + 1.0 * jax.random.uniform(key_list[7], (N_SECTION, D), jnp.float32) ** block_scale(key_list[7], (N_SECTION, D), ((0, 2),), -0.2, 0.2), 0.5, 1.5)
    ffn_gain = jnp.clip(0.5 + 1.0 * jax.random.uniform(key_list[8], (N_SECTION, D), jnp.float32) ** block_scale(key_list[8], (N_SECTION, D), ((0, 2),), -0.2, 0.2), 0.5, 1.5)
    w_gate = bell_draw(key_list[9], (N_SECTION, D, EXPERTS * FF), D ** -0.5, 0.1875, ((0, 2), (2, 16)))
    w_up = bell_draw(key_list[10], (N_SECTION, D, EXPERTS * FF), D ** -0.5, 0.1875, ((0, 2), (2, 16)))
    w_down = bell_draw(key_list[11], (N_SECTION, EXPERTS * FF, D), FF ** -0.5, 0.109375, ((0, 2), (1, 16)))
    routes_keys = jax.random.split(jax.random.fold_in(key_list[12], 1), N_SECTION * REQS // BLOCK_ROWS)
    routes_turns = jax.random.permutation(jax.random.fold_in(key_list[12], 3), N_SECTION * REQS // BLOCK_ROWS)
    routes = jax.vmap(lambda own, number: assign_block(jax.random.fold_in(key_list[12], 2), own, number, BLOCK_ROWS, EXPERTS, 2, CAPACITY, 2))(routes_keys, routes_turns).reshape((N_SECTION, REQS, 2))
    gates = jnp.clip(0.25 + 0.75 * jax.random.uniform(key_list[13], (N_SECTION, REQS, 2), jnp.float32) ** block_scale(key_list[13], (N_SECTION, REQS, 2), ((0, 2), (1, 4)), -0.2, 0.2), 0.25, 1.0).astype(jnp.bfloat16)
    return {"tokens": tokens, "deal": deal, "lengths": lengths, "cache_keys": cache_keys, "cache_values": cache_values, "w_qkv": w_qkv, "w_out": w_out, "attn_gain": attn_gain, "ffn_gain": ffn_gain, "w_gate": w_gate, "w_up": w_up, "w_down": w_down, "routes": routes, "gates": gates}


epsilon = 1e-06

def rms_scale(values, gain_row):
    mean_square = lax.optimization_barrier(jnp.mean(values * values, axis=-1, keepdims=True))
    return values * lax.rsqrt(mean_square + epsilon) * gain_row

def attend_block(arguments):
    queries, new_keys, new_values, key_cache, value_cache, lengths = arguments
    score_scale = 1.0 / math.sqrt(HEAD_DIM)
    scores = jnp.einsum('bhd,bjhd->bhj', queries.astype(jnp.float32), key_cache.astype(jnp.float32)) * score_scale
    own_score = lax.optimization_barrier(jnp.sum(queries.astype(jnp.float32) * new_keys.astype(jnp.float32), axis=-1)) * score_scale
    positions = jnp.arange(CONTEXT).astype(jnp.int32)
    in_range = positions[None, None, :] < lengths.astype(jnp.int32)[:, None, None]
    scores = jnp.where(in_range, scores, -jnp.inf)
    peak_score = jnp.maximum(lax.optimization_barrier(jnp.max(scores, axis=-1)), own_score)
    cache_weight = jnp.exp(scores - peak_score[..., None])
    own_weight = jnp.exp(own_score - peak_score)
    denominator = lax.optimization_barrier(jnp.sum(cache_weight, axis=-1)) + own_weight
    cache_prob = (cache_weight / denominator[..., None]).astype(jnp.bfloat16)
    own_prob = (own_weight / denominator).astype(jnp.bfloat16)
    attended = jnp.einsum('bhj,bjhd->bhd', cache_prob.astype(jnp.float32), value_cache.astype(jnp.float32))
    attended = attended + own_prob.astype(jnp.float32)[..., None] * new_values.astype(jnp.float32)
    return attended.astype(jnp.bfloat16)

def run_layer(stream, lengths, key_cache, value_cache, qkv_weight, out_weight, attn_gain, ffn_gain, gate_weight, up_weight, down_weight, route_ids, gate_values):
    row_count = stream.shape[0]
    head_cols = HEADS * HEAD_DIM
    normed = rms_scale(stream.astype(jnp.float32), attn_gain).astype(jnp.bfloat16)
    projected = jnp.dot(normed, qkv_weight.reshape(D, 3 * head_cols), preferred_element_type=jnp.float32).astype(jnp.bfloat16)
    queries = projected[:, :head_cols].reshape(row_count, HEADS, HEAD_DIM)
    new_keys = projected[:, head_cols:2 * head_cols].reshape(row_count, HEADS, HEAD_DIM)
    new_values = projected[:, 2 * head_cols:].reshape(row_count, HEADS, HEAD_DIM)
    group_count = row_count // REQ_DEV

    def grouped(tensor):
        return tensor.reshape((group_count, REQ_DEV) + tensor.shape[1:])
    attended = lax.map(attend_block, (grouped(queries), grouped(new_keys), grouped(new_values), grouped(key_cache.reshape(row_count, CONTEXT, HEADS, HEAD_DIM)), grouped(value_cache.reshape(row_count, CONTEXT, HEADS, HEAD_DIM)), grouped(lengths)))
    attended = attended.reshape(row_count, head_cols)
    residual = stream.astype(jnp.float32) + jnp.dot(attended, out_weight, preferred_element_type=jnp.float32)
    normed_ffn = rms_scale(residual, ffn_gain).astype(jnp.bfloat16)
    row_limit = CAPACITY * (REQS // BLOCK_ROWS)
    mixture = jnp.zeros((row_count, D), jnp.float32)
    for expert in range(EXPERTS):
        matched = route_ids == expert
        weight = lax.optimization_barrier(jnp.sum(jnp.where(matched, gate_values.astype(jnp.float32), 0.0), axis=1))
        picked = jnp.nonzero(jnp.any(matched, axis=1), size=row_limit, fill_value=row_count)[0].astype(jnp.int32)
        safe_index = jnp.minimum(picked, row_count - 1).astype(jnp.int32)
        chosen_rows = normed_ffn[safe_index]
        row_weight = jnp.where(picked < row_count, weight[safe_index], 0.0)
        gate_part = jnp.dot(chosen_rows, gate_weight[:, expert * FF:(expert + 1) * FF], preferred_element_type=jnp.float32)
        up_part = jnp.dot(chosen_rows, up_weight[:, expert * FF:(expert + 1) * FF], preferred_element_type=jnp.float32)
        hidden = (row_weight[:, None] * jax.nn.gelu(gate_part, approximate=True) * up_part).astype(jnp.bfloat16)
        partial_terms = jnp.dot(hidden, down_weight[expert * FF:(expert + 1) * FF], preferred_element_type=jnp.float32)
        mixture = mixture.at[picked].add(partial_terms, mode='drop')
    return (residual + mixture).astype(jnp.bfloat16)

def reference(tokens, deal, lengths, cache_keys, cache_values, w_qkv, w_out, attn_gain, ffn_gain, w_gate, w_up, w_down, routes, gates):
    stream = tokens[deal]
    outputs = []
    for layer_index in range(N_SECTION):
        stream = run_layer(stream, lengths[layer_index], cache_keys[layer_index], cache_values[layer_index], w_qkv[layer_index], w_out[layer_index], attn_gain[layer_index], ffn_gain[layer_index], w_gate[layer_index], w_up[layer_index], w_down[layer_index], routes[layer_index], gates[layer_index])
        outputs.append(jnp.zeros_like(stream).at[deal].set(stream))
    return jnp.stack(outputs)
```

```python
import functools
import math

import jax
import jax.numpy as jnp
from jax import lax
from jax.experimental import pallas as pl
from jax.experimental.pallas import tpu as pltpu
from jax.sharding import PartitionSpec as P

HEAD_DIM = 64
EXPERTS = 16
FF = 2816
LANES = 128
BLOCK_ROWS = 16
CAPACITY = 4
HEAD_ROWS = 16
MESH = pl.DeviceIdType.MESH


epsilon = 1e-06


def rms_scale(values, gain_row):
    mean_square = jnp.mean(values * values, axis=-1, keepdims=True)
    return values * lax.rsqrt(mean_square + epsilon) * gain_row


def column(row):
    size = row.shape[1]
    diagonal = lax.broadcasted_iota(jnp.int32, (size, size), 0) == lax.broadcasted_iota(
        jnp.int32, (size, size), 1
    )
    return jnp.sum(jnp.where(diagonal, row, 0.0), axis=1, keepdims=True)


def gathered(chosen, values):
    return lax.dot_general(
        chosen.astype(jnp.bfloat16),
        values,
        (((0,), (0,)), ((), ())),
        preferred_element_type=jnp.float32,
    )


def gelu(v):
    return 0.5 * v * (1.0 + jnp.tanh(math.sqrt(2.0 / math.pi) * (v + 0.044715 * (v * v * v))))


def batched(a, b, dims):
    return lax.dot_general(a, b, (dims, ((0,), (0,))), preferred_element_type=jnp.float32)


def attend(proj, lengths, key_cache, value_cache):
    slots, context, cols = key_cache.shape
    score_scale = 1.0 / math.sqrt(HEAD_DIM)
    queries, new_keys, new_values = (part[:, None, :] for part in proj)
    row_at = lax.broadcasted_iota(jnp.int32, (1, HEAD_ROWS, cols), 1)
    lane_at = lax.broadcasted_iota(jnp.int32, (1, HEAD_ROWS, cols), 2)
    head_mask = (lane_at // HEAD_DIM == row_at).astype(jnp.float32)
    spread = queries * head_mask
    scores = batched(spread.astype(jnp.bfloat16), key_cache[...], ((2,), (2,))) * score_scale
    own_score = jnp.sum(spread * new_keys, axis=-1, keepdims=True) * score_scale
    positions = lax.broadcasted_iota(jnp.int32, (slots, HEAD_ROWS, context), 2).astype(jnp.float32)
    limit = jnp.broadcast_to(lengths, (slots, context))[:, None, :]
    scores = jnp.where(positions < limit, scores, -jnp.inf)
    peak = jnp.maximum(jnp.max(scores, axis=-1, keepdims=True), own_score)
    cache_weight = jnp.exp(scores - peak)
    own_weight = jnp.exp(own_score - peak)
    denominator = jnp.sum(cache_weight, axis=-1, keepdims=True) + own_weight
    cache_prob = (cache_weight / denominator).astype(jnp.bfloat16)
    own_prob = (own_weight / denominator).astype(jnp.bfloat16).astype(jnp.float32)
    attended = batched(cache_prob, value_cache[...], ((2,), (1,))) + own_prob * new_values
    return jnp.sum(attended * head_mask, axis=1).astype(jnp.bfloat16)


def unfold(blocks):
    half = blocks.shape[1] // 2
    rows = blocks.shape[0] * half
    parts = [blocks[:, i * half : (i + 1) * half].reshape(rows, blocks.shape[2]) for i in range(2)]
    return jnp.concatenate(parts, axis=1)


def fold(rows, depth):
    half = rows.shape[1] // 2
    count = rows.shape[0] // depth
    parts = [rows[:, i * half : (i + 1) * half].reshape(count, depth, half) for i in range(2)]
    return jnp.concatenate(parts, axis=1)


def iota(shape, axis):
    return lax.broadcasted_iota(jnp.int32, shape, axis)


def dot(a, b):
    return jnp.dot(a, b, preferred_element_type=jnp.float32)


def to_bf16(mask):
    return mask.astype(jnp.float32).astype(jnp.bfloat16)


def kernel(
    req_count,
    head_count,
    deal_hbm,
    length_hbm,
    routes_hbm,
    gates_hbm,
    tok_hbm,
    again_hbm,
    fgain_hbm,
    wqkv_hbm,
    key_hbm,
    value_hbm,
    wout_hbm,
    wgate_hbm,
    wup_hbm,
    wdown_hbm,
    out_ref,
    deal_ref,
    length_ref,
    routes_ref,
    gates_ref,
    tok_ref,
    again_ref,
    fgain_ref,
    wqkv,
    key_cache,
    value_cache,
    wext,
    wgate,
    wup,
    wdown,
    meta_all,
    meta_prev,
    proj_all,
    tokq_all,
    stream,
    part_out,
    part_in,
    hidden,
    terms_out,
    terms_in,
    final_out,
    final_in,
    made_in,
    last,
    pick,
    spread,
    weight,
    carry,
    merge,
    final_to_ref,
    load_sem,
    meta_sem,
    prev_sem,
    proj_sem,
    tokq_sem,
    part_sem,
    terms_sem,
    final_sem,
    made_sem,
    last_sem,
):
    sec = lax.axis_index("section")
    req = lax.axis_index("req")
    head = lax.axis_index("head")
    count = req_count * head_count
    me = req * head_count + head
    slots, width = tok_ref.shape
    cols = width // head_count
    reqs = slots * req_count
    units = wgate.shape[1]
    depth = slots // BLOCK_ROWS * CAPACITY
    compact = req_count * depth
    chunk = 256 if units % 256 == 0 else units
    f32, bf16 = jnp.float32, jnp.bfloat16

    barrier = pltpu.get_barrier_semaphore()

    def greet(target):
        pl.semaphore_signal(barrier, inc=1, device_id=target, device_id_type=MESH)

    def req_peer(k):
        return (sec, lax.rem(req + k, req_count), head)

    def head_peer(k):
        return (sec, req, lax.rem(head + k, head_count))

    def each(first, last, body):
        def step(k, carry):
            body(k)
            return carry

        if last - first <= 16:
            for k in range(first, last):
                body(k)
        else:
            lax.fori_loop(first, last, step, 0)

    each(1, req_count, lambda k: greet(req_peer(k)))
    each(1, head_count, lambda k: greet(head_peer(k)))
    greet((1 - sec, req, head))

    loads = [
        pltpu.make_async_copy(src, dst, load_sem.at[i])
        for i, (src, dst) in enumerate(
            [
                (tok_hbm, tok_ref),
                (again_hbm, again_ref),
                (routes_hbm, routes_ref),
                (gates_hbm, gates_ref),
                (deal_hbm, deal_ref),
                (length_hbm, length_ref),
                (fgain_hbm, fgain_ref),
                (wqkv_hbm, wqkv),
                (key_hbm.at[0], key_cache),
                (value_hbm.at[0], value_cache),
                (wout_hbm.at[0], wext.at[pl.ds(0, cols)]),
                (wgate_hbm.at[0], wgate),
                (wup_hbm.at[0], wup),
                (wdown_hbm.at[0], wdown),
            ]
        )
    ]
    for load in loads:
        load.start()

    def offset(k):
        peer = lax.rem(me + k, count)
        return peer, peer // head_count, lax.rem(peer, head_count)

    def remote(src, dst, sems, k, target):
        return pltpu.make_async_remote_copy(
            src_ref=src,
            dst_ref=dst,
            send_sem=sems.at[0, k],
            recv_sem=sems.at[1, k],
            device_id=target,
            device_id_type=MESH,
        )

    def meta_copy(k):
        return remote(meta_all.at[req], meta_all.at[req], meta_sem, k, req_peer(k))

    def prev_copy():
        return remote(meta_all.at[req], meta_prev, prev_sem, 0, (1 - sec, req, head))

    def proj_copy(k):
        return remote(proj_all.at[req], proj_all.at[req], proj_sem, k, req_peer(k))

    mine = pl.ds(pl.multiple_of(head * cols, cols), cols)

    def tokq_copy(k):
        return remote(tok_ref.at[:, mine], tokq_all.at[req], tokq_sem, k, req_peer(k))

    def part_copy(k):
        peer, peer_req, peer_head = offset(k)
        expert = peer * units // FF
        return remote(
            part_out.at[expert], part_in.at[me], part_sem, k, (sec, peer_req, peer_head)
        )

    def terms_copy(k):
        _, peer_req, peer_head = offset(k)
        return remote(
            terms_out.at[peer_req], terms_in.at[me], terms_sem, k, (1 - sec, peer_req, peer_head)
        )

    def made_copy(k):
        peer_req = lax.rem(req + k, req_count)
        return remote(
            stream.at[:, mine], made_in.at[req], made_sem, k, (1 - sec, peer_req, head)
        )

    def final_copy(k, lane):
        peer_head = lax.rem(head + lane, head_count)
        peer_req = lax.rem(req + k, req_count)
        return remote(
            final_out.at[peer_head, peer_req],
            final_in.at[me],
            final_sem,
            lane * req_count + k,
            (sec, peer_req, peer_head),
        )

    def last_copy(k):
        return remote(last.at[head], last.at[head], last_sem, k, head_peer(k))

    for load in loads[2:6]:
        load.wait()
    routes = routes_ref[...].astype(f32)
    gates = gates_ref[...].astype(f32)
    deal_row = deal_ref[...].astype(f32)
    block_of = iota((slots, slots), 0) // BLOCK_ROWS
    earlier = to_bf16(
        (iota((slots, slots), 0) < iota((slots, slots), 1))
        & (block_of == iota((slots, slots), 1) // BLOCK_ROWS)
    )
    table = (EXPERTS * depth, slots)
    expert_at = (iota(table, 0) // depth).astype(f32)
    place_at = (iota(table, 0) % depth).astype(f32)
    named = ((routes[0:1] == expert_at) | (routes[1:2] == expert_at)).astype(f32)
    before = (iota(table, 1) // BLOCK_ROWS * CAPACITY).astype(f32)
    place = dot(named.astype(bf16), earlier) + before
    chosen = jnp.where(place == place_at, named, 0.0)
    pick[...] = chosen
    places = [
        jnp.sum(
            jnp.where(routes[k : k + 1] == expert_at, chosen * place_at, 0.0), axis=0, keepdims=True
        )
        for k in range(2)
    ]
    facts = [routes[0:1], routes[1:2], places[0], places[1], gates[0:1], gates[1:2], deal_row]
    meta_all[req] = jnp.full(meta_all.shape[1:], -1.0, f32)
    for i, fact in enumerate(facts):
        meta_all[req, i : i + 1, 0:slots] = fact
    deal = column(deal_row).astype(jnp.int32)
    lengths = column(length_ref[...].astype(f32))
    taken = to_bf16(iota((slots, reqs), 1) == deal)

    def expert_facts():
        each(1, req_count, lambda k: meta_copy(k).wait_recv())
        facts = meta_all[...]
        own = (me * units // FF).astype(f32)
        at = iota((req_count, depth, LANES), 1).astype(f32)
        first = ((facts[:, 0:1] == own) & (facts[:, 2:3] == at)).astype(f32)
        second = ((facts[:, 1:2] == own) & (facts[:, 3:4] == at)).astype(f32)
        gate = jnp.sum(first * facts[:, 4:5] + second * facts[:, 5:6], axis=-1, keepdims=True)
        leads = jnp.sum(first, axis=-1, keepdims=True)
        dest = jnp.sum((first + second) * (facts[:, 6:7] + 1.0), axis=-1, keepdims=True) - 1.0
        lead_device = (lax.rem(me * units, FF) == 0).astype(f32)
        weight[...] = jnp.broadcast_to(gate.reshape(compact, 1), weight.shape)
        carry[...] = jnp.broadcast_to(leads.reshape(compact, 1) * lead_device, carry.shape)
        return dest.reshape(compact, 1).astype(jnp.int32)

    wext[pl.ds(cols, cols)] = to_bf16(
        iota((cols, width), 1) == iota((cols, width), 0) + head * cols
    )

    def projected(values):
        normed = rms_scale(values, again_ref[...]).astype(bf16)
        return [dot(normed, wqkv[i]).astype(bf16) for i in range(3)]

    @pl.when(sec == 0)
    def _():
        loads[0].wait()
        loads[1].wait()
        loads[7].wait()
        own = projected(tok_ref[...].astype(f32))
        for i in range(3):
            proj_all[req, :, i * cols : (i + 1) * cols] = own[i]
        pl.semaphore_wait(barrier, req_count + head_count - 1)
        each(1, req_count, lambda k: proj_copy(k).start())
        each(1, req_count, lambda k: tokq_copy(k).start())
        each(1, req_count, lambda k: meta_copy(k).start())
        prev_copy().start()
        tokq_all[req] = tok_ref[:, mine]
        each(1, req_count, lambda k: proj_copy(k).wait_recv())
        dealt = dot(taken, proj_all[...].reshape(reqs, 3 * cols))
        for i in range(3):
            spread[i] = dealt[:, i * cols : (i + 1) * cols]
        each(1, req_count, lambda k: tokq_copy(k).wait_recv())
        spread[3] = dot(taken, tokq_all[...].reshape(reqs, cols))

    @pl.when(sec == 1)
    def _():
        loads[0].wait()
        loads[1].wait()
        pl.semaphore_wait(barrier, req_count + head_count - 1)
        each(1, req_count, lambda k: meta_copy(k).start())
        prev_copy().wait_recv()
        dest = expert_facts()
        onto = (iota((compact, reqs), 1) == dest).astype(f32)
        merge_to = onto.astype(bf16)
        unit = to_bf16(iota((compact, compact), 0) == iota((compact, compact), 1))
        final_to = gathered(merge_to, unit)
        prev = [column(meta_prev[i : i + 1, 0:slots]) for i in range(4)]
        lanes = (slots, count * 2 * depth)
        expert_of = (iota(lanes, 1) // (2 * depth) * units // FF).astype(f32)
        part_of = iota(lanes, 1) // depth % 2
        row_of = (iota(lanes, 1) % depth).astype(f32)
        hits = ((prev[0] == expert_of) & (prev[2] == row_of)) | (
            (prev[1] == expert_of) & (prev[3] == row_of)
        )
        for half in range(2):
            merge[half] = (hits & (part_of == half)).astype(f32)
        loads[7].wait()
        each(0, count, lambda k: terms_copy(k).wait_recv())
        arrived = terms_in[...].reshape(count * 2 * depth, width // 2)
        for half in range(2):
            stream[:, half * (width // 2) : (half + 1) * (width // 2)] = dot(
                merge[half].astype(bf16), arrived
            ).astype(bf16)
        own = projected(stream[...].astype(f32))
        for i in range(3):
            spread[i] = own[i].astype(f32)
        spread[3] = stream[:, mine].astype(f32)
        each(0, req_count, lambda k: made_copy(k).start())
        final_to_ref[...] = final_to

    for load in loads[8:11]:
        load.wait()
    attended = attend([spread[i] for i in range(3)], lengths, key_cache, value_cache)
    both = jnp.concatenate([attended, spread[3].astype(bf16)], axis=1)
    packed = dot(pick[...].astype(bf16), both).astype(bf16)
    part_out[...] = fold(dot(packed, wext[...]), depth).astype(bf16)
    each(1, count, lambda k: part_copy(k).start())
    part_in[me] = part_out[me * units // FF]

    @pl.when(sec == 0)
    def _():
        expert_facts()

    loads[6].wait()
    for load in loads[11:]:
        load.wait()
    row_weight = weight[:, 0:1]
    each(1, count, lambda k: part_copy(k).wait_recv())
    shares = part_in[...].reshape(req_count, head_count, 2 * depth, width // 2)
    residual = unfold(jnp.sum(shares.astype(f32), axis=1))
    rows = rms_scale(residual, fgain_ref[...]).astype(bf16)

    def hide(c):
        at = pl.ds(c * chunk, chunk)
        gate_part = dot(rows, wgate[:, at])
        up_part = dot(rows, wup[:, at])
        hidden[:, at] = (row_weight * gelu(gate_part) * up_part).astype(bf16)

    for c in range(units // chunk):
        hide(c)
    carried = residual * carry[:, 0:1]

    @pl.when(sec == 0)
    def _():
        done = dot(hidden[...], wdown[...]) + carried
        terms_out[...] = fold(done, depth).astype(bf16)
        each(0, count, lambda k: terms_copy(k).start())
        each(0, req_count, lambda k: made_copy(k).wait_recv())
        deal_rows = meta_all[:, 6:7, 0:slots]
        total = jnp.zeros((slots, cols), f32)
        here = (req * slots + iota((slots, slots), 0)).astype(f32)
        for k in range(req_count):
            total = total + dot(to_bf16(deal_rows[k] == here), made_in[k])
        last[head] = total.astype(bf16)

    @pl.when(sec == 1)
    def _():
        done = dot(hidden[...], wdown[...]) + carried
        sent = dot(final_to_ref[...].astype(bf16), done.astype(bf16))
        for h in range(head_count):
            part = sent[:, h * cols : (h + 1) * cols].astype(bf16)
            final_out[h] = part.reshape(req_count, slots, cols)
        for lane in range(head_count):
            each(0 if lane else 1, req_count, lambda k: final_copy(k, lane).start())
        final_in[me] = final_out[head, req]
        for lane in range(head_count):
            each(0 if lane else 1, req_count, lambda k: final_copy(k, lane).wait_recv())
        last[head] = jnp.sum(final_in[...].astype(f32), axis=0).astype(bf16)

    each(1, head_count, lambda k: last_copy(k).start())
    each(1, head_count, lambda k: last_copy(k).wait_recv())
    for h in range(head_count):
        out_ref[:, h * cols : (h + 1) * cols] = last[h].astype(out_ref.dtype)

    each(1, head_count, lambda k: last_copy(k).wait_send())
    each(1, count, lambda k: part_copy(k).wait_send())
    each(1, req_count, lambda k: meta_copy(k).wait_send())

    @pl.when(sec == 0)
    def _():
        each(1, req_count, lambda k: proj_copy(k).wait_send())
        each(1, req_count, lambda k: tokq_copy(k).wait_send())
        prev_copy().wait_send()
        each(0, count, lambda k: terms_copy(k).wait_send())

    @pl.when(sec == 1)
    def _():
        each(0, req_count, lambda k: made_copy(k).wait_send())
        for lane in range(head_count):
            each(0 if lane else 1, req_count, lambda k: final_copy(k, lane).wait_send())


def on_device(
    tokens,
    deal,
    lengths,
    cache_keys,
    cache_values,
    w_qkv,
    w_out,
    attn_gain,
    ffn_gain,
    w_gate,
    w_up,
    w_down,
    routes,
    gates,
):
    req_count = lax.axis_size("req")
    head_count = lax.axis_size("head")
    count = req_count * head_count
    slots, width = tokens.shape
    reqs = slots * req_count
    units = w_gate.shape[2]
    cols = w_out.shape[1]
    context = cache_keys.shape[2]
    depth = slots // BLOCK_ROWS * CAPACITY
    compact = req_count * depth
    bf16, f32, i32 = jnp.bfloat16, jnp.float32, jnp.int32
    vmem = pl.BlockSpec(memory_space=pltpu.VMEM)
    anywhere = pl.BlockSpec(memory_space=pl.ANY)

    def sems(n):
        return pltpu.SemaphoreType.DMA((2, n))

    out = pl.pallas_call(
        functools.partial(kernel, req_count, head_count),
        out_shape=jax.ShapeDtypeStruct((slots, width), f32),
        in_specs=[anywhere] * 14,
        out_specs=vmem,
        scratch_shapes=[
            pltpu.VMEM((1, slots), i32),
            pltpu.VMEM((1, slots), i32),
            pltpu.VMEM((2, slots), i32),
            pltpu.VMEM((2, slots), bf16),
            pltpu.VMEM((slots, width), bf16),
            pltpu.VMEM((1, width), f32),
            pltpu.VMEM((1, width), f32),
            pltpu.VMEM((3, width, cols), bf16),
            pltpu.VMEM((slots, context, cols), bf16),
            pltpu.VMEM((slots, context, cols), bf16),
            pltpu.VMEM((2 * cols, width), bf16),
            pltpu.VMEM((width, units), bf16),
            pltpu.VMEM((width, units), bf16),
            pltpu.VMEM((units, width), bf16),
            pltpu.VMEM((req_count, 8, LANES), f32),
            pltpu.VMEM((8, LANES), f32),
            pltpu.VMEM((req_count, slots, 3 * cols), bf16),
            pltpu.VMEM((req_count, slots, cols), bf16),
            pltpu.VMEM((slots, width), bf16),
            pltpu.VMEM((EXPERTS, 2 * depth, width // 2), bf16),
            pltpu.VMEM((count, 2 * depth, width // 2), bf16),
            pltpu.VMEM((compact, units), bf16),
            pltpu.VMEM((req_count, 2 * depth, width // 2), bf16),
            pltpu.VMEM((count, 2 * depth, width // 2), bf16),
            pltpu.VMEM((head_count, req_count, slots, cols), bf16),
            pltpu.VMEM((count, slots, cols), bf16),
            pltpu.VMEM((req_count, slots, cols), bf16),
            pltpu.VMEM((head_count, slots, cols), bf16),
            pltpu.VMEM((EXPERTS * depth, slots), f32),
            pltpu.VMEM((4, slots, cols), f32),
            pltpu.VMEM((compact, LANES), f32),
            pltpu.VMEM((compact, LANES), f32),
            pltpu.VMEM((2, slots, count * 2 * depth), f32),
            pltpu.VMEM((reqs, compact), f32),
            pltpu.SemaphoreType.DMA((14,)),
            sems(req_count),
            sems(1),
            sems(req_count),
            sems(req_count),
            sems(count),
            sems(count),
            sems(count),
            sems(req_count),
            sems(head_count),
        ],
        compiler_params=pltpu.CompilerParams(
            collective_id=0, has_side_effects=True, vmem_limit_bytes=56 * 1024 * 1024
        ),
    )(
        deal[None],
        lengths,
        routes[0].T,
        gates[0].T,
        tokens,
        attn_gain,
        ffn_gain,
        w_qkv[0].transpose(1, 0, 2),
        cache_keys,
        cache_values,
        w_out,
        w_gate,
        w_up,
        w_down,
    )
    return out.astype(bf16)[None]


def solution(mesh):
    return jax.shard_map(
        on_device,
        mesh=mesh,
        in_specs=(
            P("req", None),
            P("req"),
            P("section", "req"),
            P("section", "req", None, "head"),
            P("section", "req", None, "head"),
            P("section", None, None, "head"),
            P("section", "head", None),
            P("section", None),
            P("section", None),
            P("section", None, ("req", "head")),
            P("section", None, ("req", "head")),
            P("section", ("req", "head"), None),
            P("section", "req", None),
            P("section", "req", None),
        ),
        out_specs=P("section", "req", None),
        check_vma=False,
    )
```

```python
import functools
import math

import jax
import jax.numpy as jnp
from jax import lax
from jax.experimental import pallas as pl
from jax.experimental.pallas import tpu as pltpu
from jax.sharding import PartitionSpec as P

HEAD_DIM = 64
EXPERTS = 16
FF = 2816
LANES = 128
BLOCK_ROWS = 16
CAPACITY = 4
HEAD_ROWS = 8
PARTS = 2
MESH = pl.DeviceIdType.MESH


epsilon = 1e-06


def rms_scale(values, gain_row):
    mean_square = jnp.mean(values * values, axis=-1, keepdims=True)
    return values * lax.rsqrt(mean_square + epsilon) * gain_row


def column(row):
    size = row.shape[1]
    diagonal = lax.broadcasted_iota(jnp.int32, (size, size), 0) == lax.broadcasted_iota(
        jnp.int32, (size, size), 1
    )
    return jnp.sum(jnp.where(diagonal, row, 0.0), axis=1, keepdims=True)


def gathered(chosen, values):
    return lax.dot_general(
        chosen.astype(jnp.bfloat16),
        values,
        (((0,), (0,)), ((), ())),
        preferred_element_type=jnp.float32,
    )


def gelu(v):
    return 0.5 * v * (1.0 + jnp.tanh(math.sqrt(2.0 / math.pi) * (v + 0.044715 * (v * v * v))))


def batched(a, b, dims):
    return lax.dot_general(a, b, (dims, ((0,), (0,))), preferred_element_type=jnp.float32)


def head_rows(cols):
    shape = (1, HEAD_ROWS, cols)
    return (iota(shape, 2) // HEAD_DIM == iota(shape, 1)).astype(jnp.float32)


def fold(rows, depth):
    half = rows.shape[1] // 2
    count = rows.shape[0] // depth
    parts = [rows[:, i * half : (i + 1) * half].reshape(count, depth, half) for i in range(2)]
    return jnp.concatenate(parts, axis=1)


def iota(shape, axis):
    return lax.broadcasted_iota(jnp.int32, shape, axis)


def dot(a, b):
    return jnp.dot(a, b, preferred_element_type=jnp.float32)


def to_bf16(mask):
    return mask.astype(jnp.float32).astype(jnp.bfloat16)


def kernel(
    req_count,
    head_count,
    deal_hbm,
    length_hbm,
    routes_hbm,
    gates_hbm,
    tok_hbm,
    again_hbm,
    fgain_hbm,
    wqkv_hbm,
    key_hbm,
    value_hbm,
    wout_hbm,
    wgate_hbm,
    wup_hbm,
    wdown_hbm,
    out_ref,
    deal_ref,
    length_ref,
    routes_ref,
    gates_ref,
    tok_ref,
    again_ref,
    fgain_ref,
    wqkv,
    key_cache,
    value_cache,
    wout,
    wgate,
    wup,
    wdown,
    meta_all,
    meta_prev,
    query_all,
    rest_all,
    tokq_all,
    stream,
    bias,
    part_out,
    part_in,
    hidden,
    terms_out,
    terms_in,
    final_out,
    final_in,
    made_in,
    last,
    pick,
    spread,
    held,
    weight,
    carry,
    carried,
    merge,
    final_to,
    load_sem,
    meta_sem,
    prev_sem,
    query_sem,
    rest_sem,
    wout_sem,
    near_sem,
    relay_sem,
    tokq_sem,
    part_sem,
    terms_sem,
    final_sem,
    made_sem,
    last_sem,
    turn_sem,
):
    sec = lax.axis_index("section")
    req = lax.axis_index("req")
    head = lax.axis_index("head")
    count = req_count * head_count
    me = req * head_count + head
    slots, width = tok_ref.shape
    cols = width // head_count
    reqs = slots * req_count
    units = wgate.shape[1]
    depth = slots // BLOCK_ROWS * CAPACITY
    compact = req_count * depth
    context = key_cache.shape[1]
    chunk = 256 if units % 256 == 0 else units
    f32, bf16 = jnp.float32, jnp.bfloat16

    barrier = pltpu.get_barrier_semaphore()

    def greet(target):
        pl.semaphore_signal(barrier, inc=1, device_id=target, device_id_type=MESH)

    def req_peer(k):
        return (sec, lax.rem(req + k, req_count), head)

    def head_peer(k):
        return (sec, req, lax.rem(head + k, head_count))

    def each(first, last, body):
        def step(k, carry):
            body(k)
            return carry

        if last - first <= 16:
            for k in range(first, last):
                body(k)
        else:
            lax.fori_loop(first, last, step, 0)

    each(1, req_count, lambda k: greet(req_peer(k)))
    each(1, head_count, lambda k: greet(head_peer(k)))
    greet((1 - sec, req, head))

    loads = [
        pltpu.make_async_copy(src, dst, load_sem.at[i])
        for i, (src, dst) in enumerate(
            [
                (tok_hbm, tok_ref),
                (again_hbm, again_ref),
                (routes_hbm, routes_ref),
                (gates_hbm, gates_ref),
                (deal_hbm, deal_ref),
                (length_hbm, length_ref),
                (fgain_hbm, fgain_ref),
                (wqkv_hbm, wqkv),
                (wout_hbm.at[0], wout.at[head]),
                (key_hbm.at[0], key_cache),
                (value_hbm.at[0], value_cache),
                (wgate_hbm.at[0], wgate),
                (wup_hbm.at[0], wup),
                (wdown_hbm.at[0], wdown),
            ]
        )
    ]
    for load in loads:
        load.start()

    def offset(k):
        peer = lax.rem(me + k, count)
        return peer, peer // head_count, lax.rem(peer, head_count)

    def remote(src, dst, sems, k, target):
        return pltpu.make_async_remote_copy(
            src_ref=src,
            dst_ref=dst,
            send_sem=sems.at[0, k],
            recv_sem=sems.at[1, k],
            device_id=target,
            device_id_type=MESH,
        )

    def meta_copy(k):
        return remote(meta_all.at[req], meta_all.at[req], meta_sem, k, req_peer(k))

    def prev_copy():
        return remote(meta_all.at[req], meta_prev, prev_sem, 0, (1 - sec, req, head))

    def query_copy(k):
        return remote(query_all.at[req], query_all.at[req], query_sem, k, req_peer(k))

    def rest_copy(k):
        return remote(rest_all.at[req], rest_all.at[req], rest_sem, k, req_peer(k))

    def wout_copy(k):
        return remote(wout.at[head], wout.at[head], wout_sem, k, head_peer(k))

    relayed = head_count == 4
    near = (head + 1 - 2 * lax.rem(head, 2), lax.rem(head + 2, head_count))

    def near_copy(i, half):
        at = wout.at[head, pl.ds(half * (cols // 2), cols // 2)]
        return remote(at, at, near_sem, 2 * i + half, (sec, req, near[i]))

    def relay_copy(i):
        at = wout.at[near[i], pl.ds(i * (cols // 2), cols // 2)]
        return remote(at, at, relay_sem, i, (sec, req, near[1 - i]))

    def each_near(body):
        for i, half in [(0, 0), (1, 1), (0, 1), (1, 0)]:
            body(i, half)

    mine = pl.ds(pl.multiple_of(head * cols, cols), cols)

    def tokq_copy(k):
        return remote(tok_ref.at[:, mine], tokq_all.at[req], tokq_sem, k, req_peer(k))

    def part_copy(k):
        peer, peer_req, peer_head = offset(k)
        expert = peer * units // FF
        return remote(
            part_out.at[expert], part_in.at[me], part_sem, k, (sec, peer_req, peer_head)
        )

    def terms_copy(k, part):
        _, peer_req, peer_head = offset(k)
        return remote(
            terms_out.at[part, peer_req],
            terms_in.at[part, me],
            terms_sem,
            part * count + k,
            (1 - sec, peer_req, peer_head),
        )

    def made_copy(k):
        peer_req = lax.rem(req + k, req_count)
        return remote(
            stream.at[:, mine], made_in.at[req], made_sem, k, (1 - sec, peer_req, head)
        )

    def final_copy(k, lane):
        peer_head = lax.rem(head + lane, head_count)
        peer_req = lax.rem(req + k, req_count)
        return remote(
            final_out.at[lane, peer_req],
            final_in.at[me],
            final_sem,
            lane * req_count + k,
            (sec, peer_req, peer_head),
        )

    def last_copy(k):
        return remote(last.at[head], last.at[head], last_sem, k, head_peer(k))

    def routing():
        for load in loads[2:6]:
            load.wait()
        routes = routes_ref[...].astype(f32)
        gates = gates_ref[...].astype(f32)
        deal_row = deal_ref[...].astype(f32)
        block_of = iota((slots, slots), 0) // BLOCK_ROWS
        earlier = to_bf16(
            (iota((slots, slots), 0) < iota((slots, slots), 1))
            & (block_of == iota((slots, slots), 1) // BLOCK_ROWS)
        )
        table = (EXPERTS * depth, slots)
        expert_at = (iota(table, 0) // depth).astype(f32)
        place_at = (iota(table, 0) % depth).astype(f32)
        named = ((routes[0:1] == expert_at) | (routes[1:2] == expert_at)).astype(f32)
        before = (iota(table, 1) // BLOCK_ROWS * CAPACITY).astype(f32)
        place = dot(named.astype(bf16), earlier) + before
        chosen = jnp.where(place == place_at, named, 0.0)
        pick[...] = chosen
        places = [
            jnp.sum(
                jnp.where(routes[k : k + 1] == expert_at, chosen * place_at, 0.0), axis=0, keepdims=True
            )
            for k in range(2)
        ]
        facts = [routes[0:1], routes[1:2], places[0], places[1], gates[0:1], gates[1:2], deal_row]
        meta_all[req] = jnp.full(meta_all.shape[1:], -1.0, f32)
        for i, fact in enumerate(facts):
            meta_all[req, i : i + 1, 0:slots] = fact
        deal = column(deal_row).astype(jnp.int32)
        lengths = column(length_ref[...].astype(f32))
        held[...] = (iota((slots, reqs), 1) == deal).astype(f32)
        at = iota((slots, context), 1).astype(f32)
        bias[...] = jnp.where(at < lengths, 0.0, -jnp.inf)
        each(1, req_count, lambda k: meta_copy(k).start())

    def expert_facts():
        each(1, req_count, lambda k: meta_copy(k).wait_recv())
        facts = meta_all[...]
        own = (me * units // FF).astype(f32)
        at = iota((req_count, depth, LANES), 1).astype(f32)
        first = ((facts[:, 0:1] == own) & (facts[:, 2:3] == at)).astype(f32)
        second = ((facts[:, 1:2] == own) & (facts[:, 3:4] == at)).astype(f32)
        gate = jnp.sum(first * facts[:, 4:5] + second * facts[:, 5:6], axis=-1, keepdims=True)
        leads = jnp.sum(first, axis=-1, keepdims=True)
        dest = jnp.sum((first + second) * (facts[:, 6:7] + 1.0), axis=-1, keepdims=True) - 1.0
        lead_device = (lax.rem(me * units, FF) == 0).astype(f32)
        weight[...] = jnp.broadcast_to(gate.reshape(compact, 1), weight.shape)
        carry[...] = jnp.broadcast_to(leads.reshape(compact, 1) * lead_device, carry.shape)
        return dest.reshape(compact, 1).astype(jnp.int32)

    def projected(values):
        normed = rms_scale(values, again_ref[...]).astype(bf16)
        return [dot(normed, wqkv[i]).astype(bf16) for i in range(3)]

    head_mask = head_rows(cols)
    loads[0].wait()
    loads[1].wait()

    @pl.when(sec == 0)
    def _():
        loads[7].wait()
        own = projected(tok_ref[...].astype(f32))
        query_all[req] = own[0]
        rest_all[req, :, 0:cols] = own[1]
        rest_all[req, :, cols : 2 * cols] = own[2]
        pl.semaphore_wait(barrier, req_count + head_count - 1)
        each(1, req_count, lambda k: query_copy(k).start())
        each(1, req_count, lambda k: rest_copy(k).start())
        each(1, req_count, lambda k: tokq_copy(k).start())
        loads[8].wait()
        if relayed:
            each_near(lambda i, half: near_copy(i, half).start())
        else:
            each(1, head_count, lambda k: wout_copy(k).start())
        tokq_all[req] = tok_ref[:, mine]
        routing()
        prev_copy().start()
        for load in loads[9:11]:
            load.wait()
        each(1, req_count, lambda k: query_copy(k).wait_recv())
        spread[0] = dot(held[...].astype(bf16), query_all[...].reshape(reqs, cols))

    @pl.when(sec == 1)
    def _():
        pl.semaphore_wait(barrier, req_count + head_count - 1)
        routing()
        prev_copy().wait_recv()
        dest = expert_facts()
        onto = to_bf16(iota((compact, reqs), 1) == dest)
        unit = to_bf16(iota((compact, compact), 0) == iota((compact, compact), 1))
        final_to[...] = gathered(onto, unit)
        prev = [column(meta_prev[i : i + 1, 0:slots]) for i in range(4)]
        lanes = (slots, count * 2 * depth)
        expert_of = (iota(lanes, 1) // (2 * depth) * units // FF).astype(f32)
        part_of = iota(lanes, 1) // depth % 2
        row_of = (iota(lanes, 1) % depth).astype(f32)
        hits = ((prev[0] == expert_of) & (prev[2] == row_of)) | (
            (prev[1] == expert_of) & (prev[3] == row_of)
        )
        for half in range(2):
            merge[half] = (hits & (part_of == half)).astype(f32)
        for load in loads[7:11]:
            load.wait()
        pl.semaphore_wait(turn_sem, 1)
        each(1, head_count, lambda k: wout_copy(k).start())
        piece = width // (2 * PARTS)
        for part in range(PARTS):
            each(0, count, lambda k: terms_copy(k, part).wait_recv())
            arrived = terms_in[part].reshape(count * 2 * depth, piece)
            for half in range(2):
                at = (2 * part + half) * piece
                stream[:, at : at + piece] = dot(merge[half].astype(bf16), arrived).astype(bf16)
        own = projected(stream[...].astype(f32))
        for i in range(3):
            spread[i] = own[i].astype(f32)
        spread[3] = stream[:, mine].astype(f32)
        each(0, req_count, lambda k: made_copy(k).start())

    asked = spread[0][:, None, :] * (head_mask / math.sqrt(HEAD_DIM))
    scores = batched(asked.astype(bf16), key_cache[...], ((2,), (2,))) + bias[...][:, None, :]

    @pl.when(sec == 0)
    def _():
        each(1, req_count, lambda k: rest_copy(k).wait_recv())
        dealt = dot(held[...].astype(bf16), rest_all[...].reshape(reqs, 2 * cols))
        spread[1] = dealt[:, 0:cols]
        spread[2] = dealt[:, cols : 2 * cols]
        each(1, req_count, lambda k: tokq_copy(k).wait_recv())
        if relayed:
            for i in range(2):
                near_copy(i, i).wait_recv()
                relay_copy(i).start()
        spread[3] = dot(held[...].astype(bf16), tokq_all[...].reshape(reqs, cols))

    own_score = jnp.sum(asked * spread[1][:, None, :], axis=-1, keepdims=True)
    peak = jnp.maximum(jnp.max(scores, axis=-1, keepdims=True), own_score)
    cache_weight = jnp.exp(scores - peak)
    own_weight = jnp.exp(own_score - peak)
    share = 1.0 / (jnp.sum(cache_weight, axis=-1, keepdims=True) + own_weight)
    cache_prob = (cache_weight * share).astype(bf16)
    own_prob = (own_weight * share).astype(bf16).astype(f32)
    mixed = batched(cache_prob, value_cache[...], ((2,), (1,))) + own_prob * spread[2][:, None, :]
    attended = jnp.sum(mixed * head_mask, axis=1)
    both = jnp.concatenate([attended.astype(bf16), spread[3].astype(bf16)], axis=1)
    part_out[...] = fold(dot(pick[...].astype(bf16), both), depth).astype(bf16)
    each(1, count, lambda k: part_copy(k).start())
    part_in[me] = part_out[me * units // FF]

    @pl.when(sec == 0)
    def _():
        expert_facts()

    loads[6].wait()
    for load in loads[11:]:
        load.wait()
    row_weight = weight[:, 0:1]
    @pl.when(sec == 0)
    def _():
        if relayed:
            for i in range(2):
                near_copy(i, 1 - i).wait_recv()
                relay_copy(i).wait_recv()
        else:
            each(1, head_count, lambda k: wout_copy(k).wait_recv())

    @pl.when(sec == 1)
    def _():
        each(1, head_count, lambda k: wout_copy(k).wait_recv())

    each(1, count, lambda k: part_copy(k).wait_recv())

    @pl.when(sec == 0)
    def _():
        pl.semaphore_signal(turn_sem, inc=1, device_id=(1, req, head), device_id_type=MESH)

    shares = part_in[...].astype(f32).reshape(req_count, head_count, 2 * depth, cols)

    def joined(first):
        parts = [
            shares[:, h, first : first + depth].reshape(compact, cols) for h in range(head_count)
        ]
        return jnp.concatenate(parts, axis=1)

    residual = joined(depth) + dot(joined(0).astype(bf16), wout[...].reshape(width, width))
    rows = rms_scale(residual, fgain_ref[...]).astype(bf16)

    def hide(c):
        at = pl.ds(c * chunk, chunk)
        gate_part = dot(rows, wgate[:, at])
        up_part = dot(rows, wup[:, at])
        hidden[:, at] = (row_weight * gelu(gate_part) * up_part).astype(bf16)

    for c in range(units // chunk):
        hide(c)
    carried[...] = residual * carry[:, 0:1]

    @pl.when(sec == 0)
    def _():
        for part in range(PARTS):
            at = pl.ds(part * (width // PARTS), width // PARTS)
            done = dot(hidden[...], wdown[:, at]) + carried[:, at]
            terms_out[part] = fold(done, depth).astype(bf16)
            each(0, count, lambda k: terms_copy(k, part).start())
        each(0, req_count, lambda k: made_copy(k).wait_recv())
        deal_rows = meta_all[:, 6:7, 0:slots]
        total = jnp.zeros((slots, cols), f32)
        here = (req * slots + iota((slots, slots), 0)).astype(f32)
        for k in range(req_count):
            total = total + dot(to_bf16(deal_rows[k] == here), made_in[k])
        last[head] = total.astype(bf16)

    @pl.when(sec == 1)
    def _():
        for lane in [*range(1, head_count), 0]:
            to = lax.rem(head + lane, head_count)
            at = pl.ds(pl.multiple_of(to * cols, cols), cols)
            done = dot(hidden[...], wdown[:, at]) + carried[:, at]
            sent = dot(final_to[...].astype(bf16), done.astype(bf16))
            final_out[lane] = sent.astype(bf16).reshape(req_count, slots, cols)
            each(0 if lane else 1, req_count, lambda k: final_copy(k, lane).start())
        final_in[me] = final_out[0, req]
        for lane in range(head_count):
            each(0 if lane else 1, req_count, lambda k: final_copy(k, lane).wait_recv())
        last[head] = jnp.sum(final_in[...].astype(f32), axis=0).astype(bf16)

    each(1, head_count, lambda k: last_copy(k).start())
    each(1, head_count, lambda k: last_copy(k).wait_recv())
    for h in range(head_count):
        out_ref[:, h * cols : (h + 1) * cols] = last[h].astype(out_ref.dtype)

    each(1, head_count, lambda k: last_copy(k).wait_send())
    each(1, count, lambda k: part_copy(k).wait_send())
    each(1, req_count, lambda k: meta_copy(k).wait_send())

    @pl.when(sec == 0)
    def _():
        each(1, req_count, lambda k: query_copy(k).wait_send())
        each(1, req_count, lambda k: rest_copy(k).wait_send())
        each(1, req_count, lambda k: tokq_copy(k).wait_send())
        prev_copy().wait_send()
        if relayed:
            each_near(lambda i, half: near_copy(i, half).wait_send())
            for i in range(2):
                relay_copy(i).wait_send()
        else:
            each(1, head_count, lambda k: wout_copy(k).wait_send())
        for part in range(PARTS):
            each(0, count, lambda k: terms_copy(k, part).wait_send())

    @pl.when(sec == 1)
    def _():
        each(1, head_count, lambda k: wout_copy(k).wait_send())
        each(0, req_count, lambda k: made_copy(k).wait_send())
        for lane in range(head_count):
            each(0 if lane else 1, req_count, lambda k: final_copy(k, lane).wait_send())


def on_device(
    tokens,
    deal,
    lengths,
    cache_keys,
    cache_values,
    w_qkv,
    w_out,
    attn_gain,
    ffn_gain,
    w_gate,
    w_up,
    w_down,
    routes,
    gates,
):
    req_count = lax.axis_size("req")
    head_count = lax.axis_size("head")
    count = req_count * head_count
    slots, width = tokens.shape
    reqs = slots * req_count
    units = w_gate.shape[2]
    cols = w_out.shape[1]
    context = cache_keys.shape[2]
    depth = slots // BLOCK_ROWS * CAPACITY
    compact = req_count * depth
    bf16, f32, i32 = jnp.bfloat16, jnp.float32, jnp.int32
    vmem = pl.BlockSpec(memory_space=pltpu.VMEM)
    anywhere = pl.BlockSpec(memory_space=pl.ANY)

    def sems(n):
        return pltpu.SemaphoreType.DMA((2, n))

    out = pl.pallas_call(
        functools.partial(kernel, req_count, head_count),
        out_shape=pltpu.VMEM((slots, width), f32),
        in_specs=[anywhere] * 14,
        out_specs=vmem,
        scratch_shapes=[
            pltpu.VMEM((1, slots), i32),
            pltpu.VMEM((1, slots), i32),
            pltpu.VMEM((2, slots), i32),
            pltpu.VMEM((2, slots), bf16),
            pltpu.VMEM((slots, width), bf16),
            pltpu.VMEM((1, width), f32),
            pltpu.VMEM((1, width), f32),
            pltpu.VMEM((3, width, cols), bf16),
            pltpu.VMEM((slots, context, cols), bf16),
            pltpu.VMEM((slots, context, cols), bf16),
            pltpu.VMEM((head_count, cols, width), bf16),
            pltpu.VMEM((width, units), bf16),
            pltpu.VMEM((width, units), bf16),
            pltpu.VMEM((units, width), bf16),
            pltpu.VMEM((req_count, 8, LANES), f32),
            pltpu.VMEM((8, LANES), f32),
            pltpu.VMEM((req_count, slots, cols), bf16),
            pltpu.VMEM((req_count, slots, 2 * cols), bf16),
            pltpu.VMEM((req_count, slots, cols), bf16),
            pltpu.VMEM((slots, width), bf16),
            pltpu.VMEM((slots, context), f32),
            pltpu.VMEM((EXPERTS, 2 * depth, cols), bf16),
            pltpu.VMEM((count, 2 * depth, cols), bf16),
            pltpu.VMEM((compact, units), bf16),
            pltpu.VMEM((PARTS, req_count, 2 * depth, width // (2 * PARTS)), bf16),
            pltpu.VMEM((PARTS, count, 2 * depth, width // (2 * PARTS)), bf16),
            pltpu.VMEM((head_count, req_count, slots, cols), bf16),
            pltpu.VMEM((count, slots, cols), bf16),
            pltpu.VMEM((req_count, slots, cols), bf16),
            pltpu.VMEM((head_count, slots, cols), bf16),
            pltpu.VMEM((EXPERTS * depth, slots), f32),
            pltpu.VMEM((4, slots, cols), f32),
            pltpu.VMEM((slots, reqs), f32),
            pltpu.VMEM((compact, LANES), f32),
            pltpu.VMEM((compact, LANES), f32),
            pltpu.VMEM((compact, width), f32),
            pltpu.VMEM((2, slots, count * 2 * depth), f32),
            pltpu.VMEM((reqs, compact), f32),
            pltpu.SemaphoreType.DMA((14,)),
            sems(req_count),
            sems(1),
            sems(req_count),
            sems(req_count),
            sems(head_count),
            sems(4),
            sems(2),
            sems(req_count),
            sems(count),
            sems(PARTS * count),
            sems(count),
            sems(req_count),
            sems(head_count),
            pltpu.SemaphoreType.REGULAR,
        ],
        compiler_params=pltpu.CompilerParams(
            collective_id=0, has_side_effects=True, vmem_limit_bytes=56 * 1024 * 1024
        ),
    )(
        deal[None],
        lengths,
        routes[0].T,
        gates[0].T,
        tokens,
        attn_gain,
        ffn_gain,
        w_qkv[0].transpose(1, 0, 2),
        cache_keys,
        cache_values,
        w_out,
        w_gate,
        w_up,
        w_down,
    )
    return out.astype(bf16)[None]


def solution(mesh):
    return jax.shard_map(
        on_device,
        mesh=mesh,
        in_specs=(
            P("req", None),
            P("req"),
            P("section", "req"),
            P("section", "req", None, "head"),
            P("section", "req", None, "head"),
            P("section", None, None, "head"),
            P("section", "head", None),
            P("section", None),
            P("section", None),
            P("section", None, ("req", "head")),
            P("section", None, ("req", "head")),
            P("section", ("req", "head"), None),
            P("section", "req", None),
            P("section", "req", None),
        ),
        out_specs=P("section", "req", None),
        check_vma=False,
    )
```

```python
import functools
import math

import jax
import jax.numpy as jnp
from jax import lax
from jax.experimental import pallas as pl
from jax.experimental.pallas import tpu as pltpu
from jax.sharding import PartitionSpec as P

HEAD_DIM = 64
EXPERTS = 16
FF = 2816
LANES = 128
BLOCK_ROWS = 16
CAPACITY = 4
HEAD_ROWS = 8
PARTS = 2
MESH = pl.DeviceIdType.MESH


epsilon = 1e-06


def rms_scale(values, gain_row):
    mean_square = jnp.mean(values * values, axis=-1, keepdims=True)
    return values * lax.rsqrt(mean_square + epsilon) * gain_row


def column(row):
    size = row.shape[1]
    diagonal = lax.broadcasted_iota(jnp.int32, (size, size), 0) == lax.broadcasted_iota(
        jnp.int32, (size, size), 1
    )
    return jnp.sum(jnp.where(diagonal, row, 0.0), axis=1, keepdims=True)


def gathered(chosen, values):
    return lax.dot_general(
        chosen.astype(jnp.bfloat16),
        values,
        (((0,), (0,)), ((), ())),
        preferred_element_type=jnp.float32,
    )


def gelu(v):
    return 0.5 * v * (1.0 + jnp.tanh(math.sqrt(2.0 / math.pi) * (v + 0.044715 * (v * v * v))))


def batched(a, b, dims):
    return lax.dot_general(a, b, (dims, ((0,), (0,))), preferred_element_type=jnp.float32)


def head_rows(cols):
    shape = (1, HEAD_ROWS, cols)
    return (iota(shape, 2) // HEAD_DIM == iota(shape, 1)).astype(jnp.float32)


def unfold(blocks):
    half = blocks.shape[1] // 2
    rows = blocks.shape[0] * half
    parts = [blocks[:, i * half : (i + 1) * half].reshape(rows, blocks.shape[2]) for i in range(2)]
    return jnp.concatenate(parts, axis=1)


def fold(rows, depth):
    half = rows.shape[1] // 2
    count = rows.shape[0] // depth
    parts = [rows[:, i * half : (i + 1) * half].reshape(count, depth, half) for i in range(2)]
    return jnp.concatenate(parts, axis=1)


def iota(shape, axis):
    return lax.broadcasted_iota(jnp.int32, shape, axis)


def dot(a, b):
    return jnp.dot(a, b, preferred_element_type=jnp.float32)


def to_bf16(mask):
    return mask.astype(jnp.float32).astype(jnp.bfloat16)


def kernel(
    req_count,
    head_count,
    deal_hbm,
    length_hbm,
    routes_hbm,
    gates_hbm,
    tok_hbm,
    again_hbm,
    fgain_hbm,
    wqkv_hbm,
    key_hbm,
    value_hbm,
    wout_hbm,
    wgate_hbm,
    wup_hbm,
    wdown_hbm,
    out_ref,
    deal_ref,
    length_ref,
    routes_ref,
    gates_ref,
    tok_ref,
    again_ref,
    fgain_ref,
    wqkv,
    key_cache,
    value_cache,
    wout,
    wgate,
    wup,
    wdown,
    meta_all,
    meta_prev,
    query_all,
    rest_all,
    tokq_all,
    stream,
    bias,
    base_out,
    base_in,
    part_out,
    part_in,
    hidden,
    terms_out,
    terms_in,
    final_out,
    final_in,
    made_in,
    last,
    pick,
    spread,
    held,
    weight,
    carry,
    carried,
    merge,
    final_to,
    load_sem,
    meta_sem,
    prev_sem,
    query_sem,
    rest_sem,
    tokq_sem,
    base_sem,
    part_sem,
    terms_sem,
    final_sem,
    made_sem,
    last_sem,
):
    sec = lax.axis_index("section")
    req = lax.axis_index("req")
    head = lax.axis_index("head")
    count = req_count * head_count
    me = req * head_count + head
    slots, width = tok_ref.shape
    cols = width // head_count
    reqs = slots * req_count
    units = wgate.shape[1]
    depth = slots // BLOCK_ROWS * CAPACITY
    compact = req_count * depth
    context = key_cache.shape[1]
    chunk = LANES if units % LANES == 0 else units
    f32, bf16 = jnp.float32, jnp.bfloat16

    barrier = pltpu.get_barrier_semaphore()

    def greet(target):
        pl.semaphore_signal(barrier, inc=1, device_id=target, device_id_type=MESH)

    def req_peer(k):
        return (sec, lax.rem(req + k, req_count), head)

    def head_peer(k):
        return (sec, req, lax.rem(head + k, head_count))

    def each(first, last, body):
        def step(k, carry):
            body(k)
            return carry

        if last - first <= 16:
            for k in range(first, last):
                body(k)
        else:
            lax.fori_loop(first, last, step, 0)

    each(1, req_count, lambda k: greet(req_peer(k)))
    each(1, head_count, lambda k: greet(head_peer(k)))
    greet((1 - sec, req, head))

    loads = [
        pltpu.make_async_copy(src, dst, load_sem.at[i])
        for i, (src, dst) in enumerate(
            [
                (tok_hbm, tok_ref),
                (again_hbm, again_ref),
                (routes_hbm, routes_ref),
                (gates_hbm, gates_ref),
                (deal_hbm, deal_ref),
                (length_hbm, length_ref),
                (fgain_hbm, fgain_ref),
                (wqkv_hbm, wqkv),
                (wout_hbm.at[0], wout),
                (key_hbm.at[0], key_cache),
                (value_hbm.at[0], value_cache),
                (wgate_hbm.at[0], wgate),
                (wup_hbm.at[0], wup),
                (wdown_hbm.at[0], wdown),
            ]
        )
    ]
    for load in loads:
        load.start()

    def remote(src, dst, sems, k, target, sender):
        return pltpu.make_async_remote_copy(
            src_ref=src,
            dst_ref=dst,
            send_sem=sems.at[0, k],
            recv_sem=sems.at[1, sender],
            device_id=target,
            device_id_type=MESH,
        )

    def far_req(k):
        if req_count != 4:
            return lax.rem(req + req_count - 1 - k, req_count)
        upper = req // 2
        inner = req + upper * (3 - 2 * req)
        to = (3, 2 - 2 * inner, 1 + inner, inner)[k]
        return to + upper * (3 - 2 * to)

    def far_head(k):
        if head_count != 4:
            return lax.rem(head + head_count - 1 - k, head_count)
        return (3 - head, lax.rem(head + 2, 4), head + 1 - 2 * lax.rem(head, 2), head)[k]

    def to_reqs(body, own=0):
        if req_count == 4:
            for k in range(req_count - 1 + own):
                body(k, far_req(k))
        else:
            each(0, req_count - 1 + own, lambda k: body(k, far_req(k)))

    def to_heads(body):
        for k in range(head_count - 1):
            body(k, far_head(k))

    def to_all(body, own=0):
        if count <= 16:
            places = [(h, r) for h in range(head_count) for r in range(req_count)]
            for k, (h, r) in enumerate(places[: count - 1 + own]):
                body(k, far_req(r), far_head(h))
        else:

            def at_offset(k):
                peer = lax.rem(me + count - 1 - k, count)
                body(k, peer // head_count, lax.rem(peer, head_count))

            each(0, count - 1 + own, at_offset)

    def from_others(index, size, body, own=0):
        each(1 - own, size, lambda k: body(lax.rem(index + k, size)))

    def meta_copy(k, to, sender):
        return remote(meta_all.at[req], meta_all.at[req], meta_sem, k, (sec, to, head), sender)

    def prev_copy():
        return remote(meta_all.at[req], meta_prev, prev_sem, 0, (1 - sec, req, head), 0)

    def query_copy(k, to, sender):
        return remote(query_all.at[req], query_all.at[req], query_sem, k, (sec, to, head), sender)

    def rest_copy(k, to, sender):
        return remote(rest_all.at[req], rest_all.at[req], rest_sem, k, (sec, to, head), sender)

    mine = pl.ds(pl.multiple_of(head * cols, cols), cols)

    def tokq_copy(k, to, sender):
        return remote(tok_ref.at[:, mine], tokq_all.at[req], tokq_sem, k, (sec, to, head), sender)

    def part_copy(k, to_req, to_head, sender):
        expert = (to_req * head_count + to_head) * units // FF
        return remote(
            part_out.at[expert], part_in.at[me], part_sem, k, (sec, to_req, to_head), sender
        )

    def base_copy(k, to_req, to_head, sender):
        expert = (to_req * head_count + to_head) * units // FF
        return remote(
            base_out.at[expert], base_in.at[me], base_sem, k, (sec, to_req, to_head), sender
        )

    def terms_copy(k, to_req, to_head, sender, part):
        return remote(
            terms_out.at[part, to_req],
            terms_in.at[part, me],
            terms_sem,
            part * count + k,
            (1 - sec, to_req, to_head),
            part * count + sender,
        )

    def made_copy(k, to, sender):
        return remote(
            stream.at[:, mine], made_in.at[req], made_sem, k, (1 - sec, to, head), sender
        )

    def final_copy(lane, k, to, to_head, sender):
        return remote(
            final_out.at[lane, to],
            final_in.at[me],
            final_sem,
            lane * req_count + k,
            (sec, to, to_head),
            sender,
        )

    def last_copy(k, to, sender):
        return remote(last.at[head], last.at[head], last_sem, k, (sec, req, to), sender)

    def begin(loop, copy, index, **more):
        loop(lambda k, *to: copy(k, *to, index).start(), **more)

    def ended(loop, copy, index, **more):
        loop(lambda k, *to: copy(k, *to, index).wait_send(), **more)

    def routing():
        for load in loads[2:6]:
            load.wait()
        routes = routes_ref[...].astype(f32)
        gates = gates_ref[...].astype(f32)
        deal_row = deal_ref[...].astype(f32)
        block_of = iota((slots, slots), 0) // BLOCK_ROWS
        earlier = to_bf16(
            (iota((slots, slots), 0) < iota((slots, slots), 1))
            & (block_of == iota((slots, slots), 1) // BLOCK_ROWS)
        )
        table = (EXPERTS * depth, slots)
        expert_at = (iota(table, 0) // depth).astype(f32)
        place_at = (iota(table, 0) % depth).astype(f32)
        named = ((routes[0:1] == expert_at) | (routes[1:2] == expert_at)).astype(f32)
        before = (iota(table, 1) // BLOCK_ROWS * CAPACITY).astype(f32)
        place = dot(named.astype(bf16), earlier) + before
        chosen = jnp.where(place == place_at, named, 0.0)
        pick[...] = chosen
        places = [
            jnp.sum(
                jnp.where(routes[k : k + 1] == expert_at, chosen * place_at, 0.0), axis=0, keepdims=True
            )
            for k in range(2)
        ]
        facts = [routes[0:1], routes[1:2], places[0], places[1], gates[0:1], gates[1:2], deal_row]
        meta_all[req] = jnp.full(meta_all.shape[1:], -1.0, f32)
        for i, fact in enumerate(facts):
            meta_all[req, i : i + 1, 0:slots] = fact
        deal = column(deal_row).astype(jnp.int32)
        lengths = column(length_ref[...].astype(f32))
        held[...] = (iota((slots, reqs), 1) == deal).astype(f32)
        at = iota((slots, context), 1).astype(f32)
        bias[...] = jnp.where(at < lengths, 0.0, -jnp.inf)
        begin(to_reqs, meta_copy, req)

    def expert_facts():
        from_others(req, req_count, lambda r: meta_copy(0, req, r).wait_recv())
        facts = meta_all[...]
        own = (me * units // FF).astype(f32)
        at = iota((req_count, depth, LANES), 1).astype(f32)
        first = ((facts[:, 0:1] == own) & (facts[:, 2:3] == at)).astype(f32)
        second = ((facts[:, 1:2] == own) & (facts[:, 3:4] == at)).astype(f32)
        gate = jnp.sum(first * facts[:, 4:5] + second * facts[:, 5:6], axis=-1, keepdims=True)
        leads = jnp.sum(first, axis=-1, keepdims=True)
        dest = jnp.sum((first + second) * (facts[:, 6:7] + 1.0), axis=-1, keepdims=True) - 1.0
        lead_device = (lax.rem(me * units, FF) == 0).astype(f32)
        weight[...] = jnp.broadcast_to(gate.reshape(compact, 1), weight.shape)
        carry[...] = jnp.broadcast_to(leads.reshape(compact, 1) * lead_device, carry.shape)
        return dest.reshape(compact, 1).astype(jnp.int32)

    def send_base(values):
        base_out[...] = fold(dot(pick[...].astype(bf16), values), depth).astype(bf16)
        begin(to_all, base_copy, me)
        base_in[me] = base_out[me * units // FF]

    def projected(values):
        normed = rms_scale(values, again_ref[...]).astype(bf16)
        return [dot(normed, wqkv[i]).astype(bf16) for i in range(3)]

    head_mask = head_rows(cols)
    loads[0].wait()
    loads[1].wait()

    @pl.when(sec == 0)
    def _():
        loads[7].wait()
        own = projected(tok_ref[...].astype(f32))
        query_all[req] = own[0]
        rest_all[req, :, 0:cols] = own[1]
        rest_all[req, :, cols : 2 * cols] = own[2]
        pl.semaphore_wait(barrier, req_count + head_count - 1)
        begin(to_reqs, query_copy, req)
        begin(to_reqs, rest_copy, req)
        begin(to_reqs, tokq_copy, req)
        tokq_all[req] = tok_ref[:, mine]
        routing()
        prev_copy().start()
        for load in loads[8:11]:
            load.wait()
        from_others(req, req_count, lambda r: query_copy(0, req, r).wait_recv())
        spread[0] = dot(held[...].astype(bf16), query_all[...].reshape(reqs, cols))

    @pl.when(sec == 1)
    def _():
        pl.semaphore_wait(barrier, req_count + head_count - 1)
        routing()
        prev_copy().wait_recv()
        dest = expert_facts()
        onto = to_bf16(iota((compact, reqs), 1) == dest)
        unit = to_bf16(iota((compact, compact), 0) == iota((compact, compact), 1))
        final_to[...] = gathered(onto, unit)
        prev = [column(meta_prev[i : i + 1, 0:slots]) for i in range(4)]
        lanes = (slots, count * 2 * depth)
        expert_of = (iota(lanes, 1) // (2 * depth) * units // FF).astype(f32)
        part_of = iota(lanes, 1) // depth % 2
        row_of = (iota(lanes, 1) % depth).astype(f32)
        hits = ((prev[0] == expert_of) & (prev[2] == row_of)) | (
            (prev[1] == expert_of) & (prev[3] == row_of)
        )
        for half in range(2):
            merge[half] = (hits & (part_of == half)).astype(f32)
        for load in loads[7:11]:
            load.wait()
        piece = width // (2 * PARTS)
        for part in range(PARTS):
            from_others(
                me, count, lambda p: terms_copy(0, req, head, p, part).wait_recv(), own=1
            )
            arrived = terms_in[part].reshape(count * 2 * depth, piece)
            for half in range(2):
                at = (2 * part + half) * piece
                stream[:, at : at + piece] = dot(merge[half].astype(bf16), arrived).astype(bf16)
        own = projected(stream[...].astype(f32))
        for i in range(3):
            spread[i] = own[i].astype(f32)
        send_base(stream[:, mine])
        begin(to_reqs, made_copy, req, own=1)

    asked = spread[0][:, None, :] * (head_mask / math.sqrt(HEAD_DIM))
    scores = batched(asked.astype(bf16), key_cache[...], ((2,), (2,))) + bias[...][:, None, :]

    @pl.when(sec == 0)
    def _():
        from_others(req, req_count, lambda r: rest_copy(0, req, r).wait_recv())
        dealt = dot(held[...].astype(bf16), rest_all[...].reshape(reqs, 2 * cols))
        spread[1] = dealt[:, 0:cols]
        spread[2] = dealt[:, cols : 2 * cols]
        from_others(req, req_count, lambda r: tokq_copy(0, req, r).wait_recv())
        send_base(dot(held[...].astype(bf16), tokq_all[...].reshape(reqs, cols)).astype(bf16))

    own_score = jnp.sum(asked * spread[1][:, None, :], axis=-1, keepdims=True)
    peak = jnp.maximum(jnp.max(scores, axis=-1, keepdims=True), own_score)
    cache_weight = jnp.exp(scores - peak)
    own_weight = jnp.exp(own_score - peak)
    share = 1.0 / (jnp.sum(cache_weight, axis=-1, keepdims=True) + own_weight)
    cache_prob = (cache_weight * share).astype(bf16)
    own_prob = (own_weight * share).astype(bf16).astype(f32)
    mixed = batched(cache_prob, value_cache[...], ((2,), (1,))) + own_prob * spread[2][:, None, :]
    attended = jnp.sum(mixed * head_mask, axis=1)
    packed = dot(pick[...].astype(bf16), attended.astype(bf16)).astype(bf16)
    part_out[...] = fold(dot(packed, wout[...]), depth).astype(bf16)
    begin(to_all, part_copy, me)
    part_in[me] = part_out[me * units // FF]

    @pl.when(sec == 0)
    def _():
        expert_facts()

    loads[6].wait()
    for load in loads[11:]:
        load.wait()
    row_weight = weight[:, 0:1]
    from_others(me, count, lambda p: base_copy(0, req, head, p).wait_recv())
    bases = base_in[...].reshape(req_count, head_count, 2 * depth, cols // 2).astype(f32)
    base = jnp.concatenate([unfold(bases[:, h]) for h in range(head_count)], axis=1)
    from_others(me, count, lambda p: part_copy(0, req, head, p).wait_recv())
    shares = part_in[...].reshape(req_count, head_count, 2 * depth, width // 2)
    residual = base + unfold(jnp.sum(shares.astype(f32), axis=1))
    rows = rms_scale(residual, fgain_ref[...]).astype(bf16)

    def hide(c):
        at = pl.ds(c * chunk, chunk)
        gate_part = dot(rows, wgate[:, at])
        up_part = dot(rows, wup[:, at])
        hidden[:, at] = (row_weight * gelu(gate_part) * up_part).astype(bf16)

    for c in range(units // chunk):
        hide(c)
    carried[...] = residual * carry[:, 0:1]

    @pl.when(sec == 0)
    def _():
        for part in range(PARTS):
            at = pl.ds(part * (width // PARTS), width // PARTS)
            done = dot(hidden[...], wdown[:, at]) + carried[:, at]
            terms_out[part] = fold(done, depth).astype(bf16)
            begin(to_all, functools.partial(terms_copy, part=part), me, own=1)
        from_others(req, req_count, lambda r: made_copy(0, req, r).wait_recv(), own=1)
        deal_rows = meta_all[:, 6:7, 0:slots]
        total = jnp.zeros((slots, cols), f32)
        here = (req * slots + iota((slots, slots), 0)).astype(f32)
        for k in range(req_count):
            total = total + dot(to_bf16(deal_rows[k] == here), made_in[k])
        last[head] = total.astype(bf16)

    @pl.when(sec == 1)
    def _():
        for lane in range(head_count):
            to_head = far_head(lane)
            at = pl.ds(pl.multiple_of(to_head * cols, cols), cols)
            done = dot(hidden[...], wdown[:, at]) + carried[:, at]
            sent = dot(final_to[...].astype(bf16), done.astype(bf16))
            final_out[lane] = sent.astype(bf16).reshape(req_count, slots, cols)
            to_reqs(
                lambda k, to: final_copy(lane, k, to, to_head, me).start(),
                own=int(lane < head_count - 1),
            )
        final_in[me] = final_out[head_count - 1, req]
        from_others(me, count, lambda p: final_copy(0, 0, req, head, p).wait_recv())
        last[head] = jnp.sum(final_in[...].astype(f32), axis=0).astype(bf16)

    begin(to_heads, last_copy, head)
    from_others(head, head_count, lambda h: last_copy(0, head, h).wait_recv())
    for h in range(head_count):
        out_ref[:, h * cols : (h + 1) * cols] = last[h].astype(out_ref.dtype)

    ended(to_heads, last_copy, head)
    ended(to_all, part_copy, me)
    ended(to_all, base_copy, me)
    ended(to_reqs, meta_copy, req)

    @pl.when(sec == 0)
    def _():
        ended(to_reqs, query_copy, req)
        ended(to_reqs, rest_copy, req)
        ended(to_reqs, tokq_copy, req)
        prev_copy().wait_send()
        for part in range(PARTS):
            ended(to_all, functools.partial(terms_copy, part=part), me, own=1)

    @pl.when(sec == 1)
    def _():
        ended(to_reqs, made_copy, req, own=1)
        for lane in range(head_count):
            to_reqs(
                lambda k, to: final_copy(lane, k, to, far_head(lane), me).wait_send(),
                own=int(lane < head_count - 1),
            )


def on_device(
    tokens,
    deal,
    lengths,
    cache_keys,
    cache_values,
    w_qkv,
    w_out,
    attn_gain,
    ffn_gain,
    w_gate,
    w_up,
    w_down,
    routes,
    gates,
):
    req_count = lax.axis_size("req")
    head_count = lax.axis_size("head")
    count = req_count * head_count
    slots, width = tokens.shape
    reqs = slots * req_count
    units = w_gate.shape[2]
    cols = w_out.shape[1]
    context = cache_keys.shape[2]
    depth = slots // BLOCK_ROWS * CAPACITY
    compact = req_count * depth
    bf16, f32, i32 = jnp.bfloat16, jnp.float32, jnp.int32
    vmem = pl.BlockSpec(memory_space=pltpu.VMEM)
    anywhere = pl.BlockSpec(memory_space=pl.ANY)

    def sems(n):
        return pltpu.SemaphoreType.DMA((2, n))

    out = pl.pallas_call(
        functools.partial(kernel, req_count, head_count),
        out_shape=pltpu.VMEM((slots, width), f32),
        in_specs=[anywhere] * 14,
        out_specs=vmem,
        scratch_shapes=[
            pltpu.VMEM((1, slots), i32),
            pltpu.VMEM((1, slots), i32),
            pltpu.VMEM((2, slots), i32),
            pltpu.VMEM((2, slots), bf16),
            pltpu.VMEM((slots, width), bf16),
            pltpu.VMEM((1, width), f32),
            pltpu.VMEM((1, width), f32),
            pltpu.VMEM((3, width, cols), bf16),
            pltpu.VMEM((slots, context, cols), bf16),
            pltpu.VMEM((slots, context, cols), bf16),
            pltpu.VMEM((cols, width), bf16),
            pltpu.VMEM((width, units), bf16),
            pltpu.VMEM((width, units), bf16),
            pltpu.VMEM((units, width), bf16),
            pltpu.VMEM((req_count, 8, LANES), f32),
            pltpu.VMEM((8, LANES), f32),
            pltpu.VMEM((req_count, slots, cols), bf16),
            pltpu.VMEM((req_count, slots, 2 * cols), bf16),
            pltpu.VMEM((req_count, slots, cols), bf16),
            pltpu.VMEM((slots, width), bf16),
            pltpu.VMEM((slots, context), f32),
            pltpu.VMEM((EXPERTS, 2 * depth, cols // 2), bf16),
            pltpu.VMEM((count, 2 * depth, cols // 2), bf16),
            pltpu.VMEM((EXPERTS, 2 * depth, width // 2), bf16),
            pltpu.VMEM((count, 2 * depth, width // 2), bf16),
            pltpu.VMEM((compact, units), bf16),
            pltpu.VMEM((PARTS, req_count, 2 * depth, width // (2 * PARTS)), bf16),
            pltpu.VMEM((PARTS, count, 2 * depth, width // (2 * PARTS)), bf16),
            pltpu.VMEM((head_count, req_count, slots, cols), bf16),
            pltpu.VMEM((count, slots, cols), bf16),
            pltpu.VMEM((req_count, slots, cols), bf16),
            pltpu.VMEM((head_count, slots, cols), bf16),
            pltpu.VMEM((EXPERTS * depth, slots), f32),
            pltpu.VMEM((3, slots, cols), f32),
            pltpu.VMEM((slots, reqs), f32),
            pltpu.VMEM((compact, LANES), f32),
            pltpu.VMEM((compact, LANES), f32),
            pltpu.VMEM((compact, width), f32),
            pltpu.VMEM((2, slots, count * 2 * depth), f32),
            pltpu.VMEM((reqs, compact), f32),
            pltpu.SemaphoreType.DMA((14,)),
            sems(req_count),
            sems(1),
            sems(req_count),
            sems(req_count),
            sems(req_count),
            sems(count),
            sems(count),
            sems(PARTS * count),
            sems(count),
            sems(req_count),
            sems(head_count),
        ],
        compiler_params=pltpu.CompilerParams(
            collective_id=0, has_side_effects=True, vmem_limit_bytes=56 * 1024 * 1024
        ),
    )(
        deal[None],
        lengths,
        routes[0].T,
        gates[0].T,
        tokens,
        attn_gain,
        ffn_gain,
        w_qkv[0].transpose(1, 0, 2),
        cache_keys,
        cache_values,
        w_out,
        w_gate,
        w_up,
        w_down,
    )
    return out.astype(bf16)[None]


def solution(mesh):
    return jax.shard_map(
        on_device,
        mesh=mesh,
        in_specs=(
            P("req", None),
            P("req"),
            P("section", "req"),
            P("section", "req", None, "head"),
            P("section", "req", None, "head"),
            P("section", None, None, "head"),
            P("section", "head", None),
            P("section", None),
            P("section", None),
            P("section", None, ("req", "head")),
            P("section", None, ("req", "head")),
            P("section", ("req", "head"), None),
            P("section", "req", None),
            P("section", "req", None),
        ),
        out_specs=P("section", "req", None),
        check_vma=False,
    )
```

```python
import functools
import math

import jax
import jax.numpy as jnp
from jax import lax
from jax.experimental import pallas as pl
from jax.experimental.pallas import tpu as pltpu
from jax.sharding import PartitionSpec as P

HEAD_DIM = 64
EXPERTS = 16
FF = 2816
LANES = 128
BLOCK_ROWS = 16
CAPACITY = 4
HEAD_ROWS = 8
PARTS = 2
MESH = pl.DeviceIdType.MESH


epsilon = 1e-06


def inverse_rms(values):
    return lax.rsqrt(jnp.mean(values * values, axis=-1, keepdims=True) + epsilon)


def column(row):
    size = row.shape[1]
    diagonal = lax.broadcasted_iota(jnp.int32, (size, size), 0) == lax.broadcasted_iota(
        jnp.int32, (size, size), 1
    )
    return jnp.sum(jnp.where(diagonal, row, 0.0), axis=1, keepdims=True)


def gathered(chosen, values):
    return lax.dot_general(
        chosen.astype(jnp.bfloat16),
        values,
        (((0,), (0,)), ((), ())),
        preferred_element_type=jnp.float32,
    )


def gelu(v):
    return 0.5 * v * (1.0 + jnp.tanh(math.sqrt(2.0 / math.pi) * (v + 0.044715 * (v * v * v))))


def batched(a, b, dims):
    return lax.dot_general(a, b, (dims, ((0,), (0,))), preferred_element_type=jnp.float32)


def head_rows(cols):
    shape = (1, HEAD_ROWS, cols)
    return (iota(shape, 2) // HEAD_DIM == iota(shape, 1)).astype(jnp.float32)


def unfold(blocks):
    half = blocks.shape[1] // 2
    rows = blocks.shape[0] * half
    parts = [blocks[:, i * half : (i + 1) * half].reshape(rows, blocks.shape[2]) for i in range(2)]
    return jnp.concatenate(parts, axis=1)


def fold(rows, depth):
    half = rows.shape[1] // 2
    count = rows.shape[0] // depth
    parts = [rows[:, i * half : (i + 1) * half].reshape(count, depth, half) for i in range(2)]
    return jnp.concatenate(parts, axis=1)


def iota(shape, axis):
    return lax.broadcasted_iota(jnp.int32, shape, axis)


def dot(a, b):
    return jnp.dot(a, b, preferred_element_type=jnp.float32)


def to_bf16(mask):
    return mask.astype(jnp.float32).astype(jnp.bfloat16)


def kernel(
    req_count,
    head_count,
    deal_hbm,
    length_hbm,
    routes_hbm,
    gates_hbm,
    tok_hbm,
    again_hbm,
    fgain_hbm,
    wqkv_hbm,
    key_hbm,
    value_hbm,
    wout_hbm,
    wgate_hbm,
    wup_hbm,
    wdown_hbm,
    out_ref,
    deal_ref,
    length_ref,
    routes_ref,
    gates_ref,
    tok_ref,
    again_ref,
    fgain_ref,
    wqkv,
    key_cache,
    value_cache,
    wout,
    wgate,
    wup,
    wdown,
    meta_all,
    meta_prev,
    query_all,
    rest_all,
    tokq_all,
    stream,
    bias,
    base_out,
    base_in,
    part_out,
    part_in,
    hidden,
    terms_out,
    terms_in,
    final_out,
    final_in,
    made_in,
    last,
    pick,
    spread,
    held,
    weight,
    carry,
    carried,
    merge,
    final_to,
    load_sem,
    meta_sem,
    prev_sem,
    query_sem,
    rest_sem,
    tokq_sem,
    base_sem,
    part_sem,
    terms_sem,
    final_sem,
    made_sem,
    last_sem,
):
    sec = lax.axis_index("section")
    req = lax.axis_index("req")
    head = lax.axis_index("head")
    count = req_count * head_count
    me = req * head_count + head
    slots, width = tok_ref.shape
    cols = width // head_count
    reqs = slots * req_count
    units = wgate.shape[1]
    depth = slots // BLOCK_ROWS * CAPACITY
    compact = req_count * depth
    context = key_cache.shape[1]
    chunk = LANES if units % LANES == 0 else units
    f32, bf16 = jnp.float32, jnp.bfloat16

    barrier = pltpu.get_barrier_semaphore()

    def greet(target):
        pl.semaphore_signal(barrier, inc=1, device_id=target, device_id_type=MESH)

    def req_peer(k):
        return (sec, lax.rem(req + k, req_count), head)

    def head_peer(k):
        return (sec, req, lax.rem(head + k, head_count))

    def each(first, last, body):
        def step(k, carry):
            body(k)
            return carry

        if last - first <= 16:
            for k in range(first, last):
                body(k)
        else:
            lax.fori_loop(first, last, step, 0)

    each(1, req_count, lambda k: greet(req_peer(k)))
    each(1, head_count, lambda k: greet(head_peer(k)))
    greet((1 - sec, req, head))

    loads = [
        pltpu.make_async_copy(src, dst, load_sem.at[i])
        for i, (src, dst) in enumerate(
            [
                (tok_hbm, tok_ref),
                (again_hbm, again_ref),
                (routes_hbm, routes_ref),
                (gates_hbm, gates_ref),
                (deal_hbm, deal_ref),
                (length_hbm, length_ref),
                (fgain_hbm, fgain_ref),
                (wqkv_hbm, wqkv),
                (wout_hbm.at[0], wout),
                (key_hbm.at[0], key_cache),
                (value_hbm.at[0], value_cache),
                (wgate_hbm.at[0], wgate),
                (wup_hbm.at[0], wup),
                (wdown_hbm.at[0], wdown),
            ]
        )
    ]
    for load in loads:
        load.start()

    def remote(src, dst, sems, k, target, sender):
        return pltpu.make_async_remote_copy(
            src_ref=src,
            dst_ref=dst,
            send_sem=sems.at[0, k],
            recv_sem=sems.at[1, sender],
            device_id=target,
            device_id_type=MESH,
        )

    def far_req(k):
        if req_count != 4:
            return lax.rem(req + req_count - 1 - k, req_count)
        upper = req // 2
        inner = req + upper * (3 - 2 * req)
        to = (3, 2 - 2 * inner, 1 + inner, inner)[k]
        return to + upper * (3 - 2 * to)

    def far_head(k):
        if head_count != 4:
            return lax.rem(head + head_count - 1 - k, head_count)
        return (3 - head, lax.rem(head + 2, 4), head + 1 - 2 * lax.rem(head, 2), head)[k]

    def to_reqs(body, own=0):
        if req_count == 4:
            for k in range(req_count - 1 + own):
                body(k, far_req(k))
        else:
            each(0, req_count - 1 + own, lambda k: body(k, far_req(k)))

    def to_heads(body):
        for k in range(head_count - 1):
            body(k, far_head(k))

    def to_all(body, own=0):
        if count <= 16:
            places = [(h, r) for h in range(head_count) for r in range(req_count)]
            for k, (h, r) in enumerate(places[: count - 1 + own]):
                body(k, far_req(r), far_head(h))
        else:

            def at_offset(k):
                peer = lax.rem(me + count - 1 - k, count)
                body(k, peer // head_count, lax.rem(peer, head_count))

            each(0, count - 1 + own, at_offset)

    def from_others(index, size, body, own=0):
        each(1 - own, size, lambda k: body(lax.rem(index + k, size)))

    def meta_copy(k, to, sender):
        return remote(meta_all.at[req], meta_all.at[req], meta_sem, k, (sec, to, head), sender)

    def prev_copy():
        return remote(meta_all.at[req], meta_prev, prev_sem, 0, (1 - sec, req, head), 0)

    def query_copy(k, to, sender):
        return remote(query_all.at[req], query_all.at[req], query_sem, k, (sec, to, head), sender)

    def rest_copy(k, to, sender):
        return remote(rest_all.at[req], rest_all.at[req], rest_sem, k, (sec, to, head), sender)

    mine = pl.ds(pl.multiple_of(head * cols, cols), cols)

    def tokq_copy(k, to, sender):
        return remote(tok_ref.at[:, mine], tokq_all.at[req], tokq_sem, k, (sec, to, head), sender)

    def part_copy(k, to_req, to_head, sender):
        expert = (to_req * head_count + to_head) * units // FF
        return remote(
            part_out.at[expert], part_in.at[me], part_sem, k, (sec, to_req, to_head), sender
        )

    def base_copy(k, to_req, to_head, sender):
        expert = (to_req * head_count + to_head) * units // FF
        return remote(
            base_out.at[expert], base_in.at[me], base_sem, k, (sec, to_req, to_head), sender
        )

    def terms_copy(k, to_req, to_head, sender, part):
        return remote(
            terms_out.at[part, to_req],
            terms_in.at[part, me],
            terms_sem,
            part * count + k,
            (1 - sec, to_req, to_head),
            part * count + sender,
        )

    def made_copy(k, to, sender):
        return remote(
            stream.at[:, mine], made_in.at[req], made_sem, k, (1 - sec, to, head), sender
        )

    def final_copy(lane, k, to, to_head, sender):
        return remote(
            final_out.at[lane, to],
            final_in.at[me],
            final_sem,
            lane * req_count + k,
            (sec, to, to_head),
            sender,
        )

    def last_copy(k, to, sender):
        return remote(last.at[head], last.at[head], last_sem, k, (sec, req, to), sender)

    def begin(loop, copy, index, **more):
        loop(lambda k, *to: copy(k, *to, index).start(), **more)

    def ended(loop, copy, index, **more):
        loop(lambda k, *to: copy(k, *to, index).wait_send(), **more)

    def routing():
        for load in loads[2:6]:
            load.wait()
        routes = routes_ref[...].astype(f32)
        gates = gates_ref[...].astype(f32)
        deal_row = deal_ref[...].astype(f32)
        block_of = iota((slots, slots), 0) // BLOCK_ROWS
        earlier = to_bf16(
            (iota((slots, slots), 0) < iota((slots, slots), 1))
            & (block_of == iota((slots, slots), 1) // BLOCK_ROWS)
        )
        table = (EXPERTS * depth, slots)
        expert_at = (iota(table, 0) // depth).astype(f32)
        place_at = (iota(table, 0) % depth).astype(f32)
        named = ((routes[0:1] == expert_at) | (routes[1:2] == expert_at)).astype(f32)
        before = (iota(table, 1) // BLOCK_ROWS * CAPACITY).astype(f32)
        place = dot(named.astype(bf16), earlier) + before
        chosen = jnp.where(place == place_at, named, 0.0)
        pick[...] = chosen
        places = [
            jnp.sum(
                jnp.where(routes[k : k + 1] == expert_at, chosen * place_at, 0.0), axis=0, keepdims=True
            )
            for k in range(2)
        ]
        facts = [routes[0:1], routes[1:2], places[0], places[1], gates[0:1], gates[1:2], deal_row]
        meta_all[req] = jnp.full(meta_all.shape[1:], -1.0, f32)
        for i, fact in enumerate(facts):
            meta_all[req, i : i + 1, 0:slots] = fact
        deal = column(deal_row).astype(jnp.int32)
        lengths = column(length_ref[...].astype(f32))
        held[...] = (iota((slots, reqs), 1) == deal).astype(f32)
        at = iota((slots, context), 1).astype(f32)
        bias[...] = jnp.where(at < lengths, 0.0, -jnp.inf)
        begin(to_reqs, meta_copy, req)

    def expert_facts():
        from_others(req, req_count, lambda r: meta_copy(0, req, r).wait_recv())
        facts = meta_all[...]
        own = (me * units // FF).astype(f32)
        at = iota((req_count, depth, LANES), 1).astype(f32)
        first = ((facts[:, 0:1] == own) & (facts[:, 2:3] == at)).astype(f32)
        second = ((facts[:, 1:2] == own) & (facts[:, 3:4] == at)).astype(f32)
        gate = jnp.sum(first * facts[:, 4:5] + second * facts[:, 5:6], axis=-1, keepdims=True)
        leads = jnp.sum(first, axis=-1, keepdims=True)
        dest = jnp.sum((first + second) * (facts[:, 6:7] + 1.0), axis=-1, keepdims=True) - 1.0
        lead_device = (lax.rem(me * units, FF) == 0).astype(f32)
        weight[...] = jnp.broadcast_to(gate.reshape(compact, 1), weight.shape)
        carry[...] = jnp.broadcast_to(leads.reshape(compact, 1) * lead_device, carry.shape)
        return dest.reshape(compact, 1).astype(jnp.int32)

    def send_base(values):
        base_out[...] = fold(dot(pick[...].astype(bf16), values), depth).astype(bf16)
        begin(to_all, base_copy, me)
        base_in[me] = base_out[me * units // FF]

    def projected(values):
        rows = (values * again_ref[...]).astype(bf16)
        scale = inverse_rms(values)
        return [(scale * dot(rows, wqkv[i])).astype(bf16) for i in range(3)]

    head_mask = head_rows(cols)
    loads[0].wait()
    loads[1].wait()

    @pl.when(sec == 0)
    def _():
        loads[7].wait()
        own = projected(tok_ref[...].astype(f32))
        query_all[req] = own[0]
        rest_all[req, :, 0:cols] = own[1]
        rest_all[req, :, cols : 2 * cols] = own[2]
        pl.semaphore_wait(barrier, req_count + head_count - 1)
        begin(to_reqs, query_copy, req)
        begin(to_reqs, rest_copy, req)
        begin(to_reqs, tokq_copy, req)
        tokq_all[req] = tok_ref[:, mine]
        routing()
        prev_copy().start()
        for load in loads[8:11]:
            load.wait()
        from_others(req, req_count, lambda r: query_copy(0, req, r).wait_recv())
        spread[0] = dot(held[...].astype(bf16), query_all[...].reshape(reqs, cols))

    @pl.when(sec == 1)
    def _():
        pl.semaphore_wait(barrier, req_count + head_count - 1)
        routing()
        prev_copy().wait_recv()
        dest = expert_facts()
        onto = to_bf16(iota((compact, reqs), 1) == dest)
        unit = to_bf16(iota((compact, compact), 0) == iota((compact, compact), 1))
        final_to[...] = gathered(onto, unit)
        prev = [column(meta_prev[i : i + 1, 0:slots]) for i in range(4)]
        lanes = (slots, count * 2 * depth)
        expert_of = (iota(lanes, 1) // (2 * depth) * units // FF).astype(f32)
        part_of = iota(lanes, 1) // depth % 2
        row_of = (iota(lanes, 1) % depth).astype(f32)
        hits = ((prev[0] == expert_of) & (prev[2] == row_of)) | (
            (prev[1] == expert_of) & (prev[3] == row_of)
        )
        for half in range(2):
            merge[half] = (hits & (part_of == half)).astype(f32)
        for load in loads[7:11]:
            load.wait()
        piece = width // (2 * PARTS)
        for part in range(PARTS):
            from_others(
                me, count, lambda p: terms_copy(0, req, head, p, part).wait_recv(), own=1
            )
            arrived = terms_in[part].reshape(count * 2 * depth, piece)
            for half in range(2):
                at = (2 * part + half) * piece
                stream[:, at : at + piece] = dot(merge[half].astype(bf16), arrived).astype(bf16)
        own = projected(stream[...].astype(f32))
        for i in range(3):
            spread[i] = own[i].astype(f32)
        send_base(stream[:, mine])

    asked = spread[0][:, None, :] * (head_mask / math.sqrt(HEAD_DIM))
    scores = batched(asked.astype(bf16), key_cache[...], ((2,), (2,))) + bias[...][:, None, :]

    @pl.when(sec == 0)
    def _():
        from_others(req, req_count, lambda r: rest_copy(0, req, r).wait_recv())
        dealt = dot(held[...].astype(bf16), rest_all[...].reshape(reqs, 2 * cols))
        spread[1] = dealt[:, 0:cols]
        spread[2] = dealt[:, cols : 2 * cols]
        from_others(req, req_count, lambda r: tokq_copy(0, req, r).wait_recv())
        send_base(dot(held[...].astype(bf16), tokq_all[...].reshape(reqs, cols)).astype(bf16))

    own_score = jnp.sum(asked * spread[1][:, None, :], axis=-1, keepdims=True)
    peak = jnp.maximum(jnp.max(scores, axis=-1, keepdims=True), own_score)
    cache_weight = jnp.exp(scores - peak)
    own_weight = jnp.exp(own_score - peak)
    share = 1.0 / (jnp.sum(cache_weight, axis=-1, keepdims=True) + own_weight)
    mixed = batched(cache_weight.astype(bf16), value_cache[...], ((2,), (1,)))
    mixed = mixed + own_weight * spread[2][:, None, :]
    attended = jnp.sum(mixed * (share * head_mask), axis=1)
    packed = dot(pick[...].astype(bf16), attended.astype(bf16)).astype(bf16)
    part_out[...] = fold(dot(packed, wout[...]), depth).astype(bf16)
    begin(to_all, part_copy, me)
    part_in[me] = part_out[me * units // FF]

    @pl.when(sec == 0)
    def _():
        expert_facts()

    @pl.when(sec == 1)
    def _():
        begin(to_reqs, made_copy, req, own=1)

    loads[6].wait()
    for load in loads[11:]:
        load.wait()
    row_weight = weight[:, 0:1]
    from_others(me, count, lambda p: base_copy(0, req, head, p).wait_recv())
    bases = base_in[...].reshape(req_count, head_count, 2 * depth, cols // 2).astype(f32)
    base = jnp.concatenate([unfold(bases[:, h]) for h in range(head_count)], axis=1)
    from_others(me, count, lambda p: part_copy(0, req, head, p).wait_recv())
    shares = part_in[...].reshape(req_count, head_count, 2 * depth, width // 2)
    residual = base + unfold(jnp.sum(shares.astype(f32), axis=1))
    rows = (residual * fgain_ref[...]).astype(bf16)
    scale = inverse_rms(residual)
    row_weight = row_weight * scale

    def hide(c):
        at = pl.ds(c * chunk, chunk)
        gate_part = dot(rows, wgate[:, at])
        up_part = dot(rows, wup[:, at])
        hidden[:, at] = (row_weight * gelu(scale * gate_part) * up_part).astype(bf16)

    for c in range(units // chunk):
        hide(c)
    carried[...] = residual * carry[:, 0:1]

    @pl.when(sec == 0)
    def _():
        for part in range(PARTS):
            at = pl.ds(part * (width // PARTS), width // PARTS)
            done = dot(hidden[...], wdown[:, at]) + carried[:, at]
            terms_out[part] = fold(done, depth).astype(bf16)
            begin(to_all, functools.partial(terms_copy, part=part), me, own=1)
        from_others(req, req_count, lambda r: made_copy(0, req, r).wait_recv(), own=1)
        deal_rows = meta_all[:, 6:7, 0:slots]
        total = jnp.zeros((slots, cols), f32)
        here = (req * slots + iota((slots, slots), 0)).astype(f32)
        for k in range(req_count):
            total = total + dot(to_bf16(deal_rows[k] == here), made_in[k])
        last[head] = total.astype(bf16)

    @pl.when(sec == 1)
    def _():
        for lane in range(head_count):
            to_head = far_head(lane)
            at = pl.ds(pl.multiple_of(to_head * cols, cols), cols)
            done = dot(hidden[...], wdown[:, at]) + carried[:, at]
            sent = dot(final_to[...].astype(bf16), done.astype(bf16))
            final_out[lane] = sent.astype(bf16).reshape(req_count, slots, cols)
            to_reqs(
                lambda k, to: final_copy(lane, k, to, to_head, me).start(),
                own=int(lane < head_count - 1),
            )
        final_in[me] = final_out[head_count - 1, req]
        from_others(me, count, lambda p: final_copy(0, 0, req, head, p).wait_recv())
        last[head] = jnp.sum(final_in[...].astype(f32), axis=0).astype(bf16)

    begin(to_heads, last_copy, head)
    from_others(head, head_count, lambda h: last_copy(0, head, h).wait_recv())
    for h in range(head_count):
        out_ref[:, h * cols : (h + 1) * cols] = last[h].astype(out_ref.dtype)

    ended(to_heads, last_copy, head)
    ended(to_all, part_copy, me)
    ended(to_all, base_copy, me)
    ended(to_reqs, meta_copy, req)

    @pl.when(sec == 0)
    def _():
        ended(to_reqs, query_copy, req)
        ended(to_reqs, rest_copy, req)
        ended(to_reqs, tokq_copy, req)
        prev_copy().wait_send()
        for part in range(PARTS):
            ended(to_all, functools.partial(terms_copy, part=part), me, own=1)

    @pl.when(sec == 1)
    def _():
        ended(to_reqs, made_copy, req, own=1)
        for lane in range(head_count):
            to_reqs(
                lambda k, to: final_copy(lane, k, to, far_head(lane), me).wait_send(),
                own=int(lane < head_count - 1),
            )


def on_device(
    tokens,
    deal,
    lengths,
    cache_keys,
    cache_values,
    w_qkv,
    w_out,
    attn_gain,
    ffn_gain,
    w_gate,
    w_up,
    w_down,
    routes,
    gates,
):
    req_count = lax.axis_size("req")
    head_count = lax.axis_size("head")
    count = req_count * head_count
    slots, width = tokens.shape
    reqs = slots * req_count
    units = w_gate.shape[2]
    cols = w_out.shape[1]
    context = cache_keys.shape[2]
    depth = slots // BLOCK_ROWS * CAPACITY
    compact = req_count * depth
    bf16, f32, i32 = jnp.bfloat16, jnp.float32, jnp.int32
    vmem = pl.BlockSpec(memory_space=pltpu.VMEM)
    anywhere = pl.BlockSpec(memory_space=pl.ANY)

    def sems(n):
        return pltpu.SemaphoreType.DMA((2, n))

    out = pl.pallas_call(
        functools.partial(kernel, req_count, head_count),
        out_shape=pltpu.VMEM((slots, width), f32),
        in_specs=[anywhere] * 14,
        out_specs=vmem,
        scratch_shapes=[
            pltpu.VMEM((1, slots), i32),
            pltpu.VMEM((1, slots), i32),
            pltpu.VMEM((2, slots), i32),
            pltpu.VMEM((2, slots), bf16),
            pltpu.VMEM((slots, width), bf16),
            pltpu.VMEM((1, width), f32),
            pltpu.VMEM((1, width), f32),
            pltpu.VMEM((3, width, cols), bf16),
            pltpu.VMEM((slots, context, cols), bf16),
            pltpu.VMEM((slots, context, cols), bf16),
            pltpu.VMEM((cols, width), bf16),
            pltpu.VMEM((width, units), bf16),
            pltpu.VMEM((width, units), bf16),
            pltpu.VMEM((units, width), bf16),
            pltpu.VMEM((req_count, 8, LANES), f32),
            pltpu.VMEM((8, LANES), f32),
            pltpu.VMEM((req_count, slots, cols), bf16),
            pltpu.VMEM((req_count, slots, 2 * cols), bf16),
            pltpu.VMEM((req_count, slots, cols), bf16),
            pltpu.VMEM((slots, width), bf16),
            pltpu.VMEM((slots, context), f32),
            pltpu.VMEM((EXPERTS, 2 * depth, cols // 2), bf16),
            pltpu.VMEM((count, 2 * depth, cols // 2), bf16),
            pltpu.VMEM((EXPERTS, 2 * depth, width // 2), bf16),
            pltpu.VMEM((count, 2 * depth, width // 2), bf16),
            pltpu.VMEM((compact, units), bf16),
            pltpu.VMEM((PARTS, req_count, 2 * depth, width // (2 * PARTS)), bf16),
            pltpu.VMEM((PARTS, count, 2 * depth, width // (2 * PARTS)), bf16),
            pltpu.VMEM((head_count, req_count, slots, cols), bf16),
            pltpu.VMEM((count, slots, cols), bf16),
            pltpu.VMEM((req_count, slots, cols), bf16),
            pltpu.VMEM((head_count, slots, cols), bf16),
            pltpu.VMEM((EXPERTS * depth, slots), f32),
            pltpu.VMEM((3, slots, cols), f32),
            pltpu.VMEM((slots, reqs), f32),
            pltpu.VMEM((compact, LANES), f32),
            pltpu.VMEM((compact, LANES), f32),
            pltpu.VMEM((compact, width), f32),
            pltpu.VMEM((2, slots, count * 2 * depth), f32),
            pltpu.VMEM((reqs, compact), f32),
            pltpu.SemaphoreType.DMA((14,)),
            sems(req_count),
            sems(1),
            sems(req_count),
            sems(req_count),
            sems(req_count),
            sems(count),
            sems(count),
            sems(PARTS * count),
            sems(count),
            sems(req_count),
            sems(head_count),
        ],
        compiler_params=pltpu.CompilerParams(
            collective_id=0, has_side_effects=True, vmem_limit_bytes=56 * 1024 * 1024
        ),
    )(
        deal[None],
        lengths,
        routes[0].T,
        gates[0].T,
        tokens,
        attn_gain,
        ffn_gain,
        w_qkv[0].transpose(1, 0, 2),
        cache_keys,
        cache_values,
        w_out,
        w_gate,
        w_up,
        w_down,
    )
    return out.astype(bf16)[None]


def solution(mesh):
    return jax.shard_map(
        on_device,
        mesh=mesh,
        in_specs=(
            P("req", None),
            P("req"),
            P("section", "req"),
            P("section", "req", None, "head"),
            P("section", "req", None, "head"),
            P("section", None, None, "head"),
            P("section", "head", None),
            P("section", None),
            P("section", None),
            P("section", None, ("req", "head")),
            P("section", None, ("req", "head")),
            P("section", ("req", "head"), None),
            P("section", "req", None),
            P("section", "req", None),
        ),
        out_specs=P("section", "req", None),
        check_vma=False,
    )
```
